128 devices in a mesh: gx: 8 (over z, core), yz: 16 (over y, x).
Axes of the slice: x: 4, y: 4, z: 4, core: 2. Of those that a mesh axis runs over, the one named last changes fastest.
Arguments:
- part_mass: float32 [128, 128, 128], P(('gx', 'yz')), may hold values from 0.2 to 2
- part_vel: float32 [128, 128, 3, 128], P(('gx', 'yz')), may hold values from -6 to 6
- corner_weight: float32 [128, 128, 8, 128], P(('gx', 'yz')), may hold values from 0 to 0.25
- corner_base: int32 [128, 128, 128], P(('gx', 'yz')), may hold values from 0 to 11774, as said below
- slot_counts: int32 [128, 128], P(('gx', 'yz')), may hold values from 1 to 128, as said below
- water_vel: float32 [3, 32, 128, 512], P(None, 'gx', 'yz'), may hold values from -12 to 12
- solid_flag: int32 [32, 128, 512], P('gx', 'yz'), may hold values from 0 to 1
Outputs:
- particle_velocity: float32 [128, 128, 3, 128], P(('gx', 'yz'))
- pressure: float32 [32, 128, 512], P('gx', 'yz')
The draws below stay inside these ranges and needn't reach their ends.
Inputs may be any that keep to these rules, and one draw needn't show every extreme that they name: corner_base is x * 8 * 512 + y * 512 + z with x < 3, y < 7, z < 511, so the whole tile lies in the block. `slot_counts`: slots below the count are live, the rest padding; in every draw some grid block receives 128 live slots from every source group.
All inputs are finite; a program needn't handle non-finite values.
Results may differ from the reference program's by a relative error of at most 0.0002.
Values sent between devices are 32-bit elements; how exact they have to be, the bound alone decides.
No kernel may reach another device: no remote copies, remote signals or barrier semaphores. Data moves between devices by JAX's collectives and lax.ppermute only.
A program may use at most 64 MiB of HBM per device.

```python
import math
import jax
import jax.numpy as jnp
from jax import lax

CX = 4
CY = 8
CZ = 512
CAP = 128
ITERS = 3
DEGREE = 3
NX = 32
NY = 128
NZ = 512
N_GX = 8
N_YZ = 16
DEVICES = 128


def draw_water_vel(key, part):
    first = jax.random.fold_in(key, 0)
    ramp = 1.0 + 2.0 * jnp.arange(NX, dtype=jnp.float32) / max(NX - 1, 1)
    ramp = ramp[None, :, None, None]
    value = jnp.clip(jax.random.normal(first, (3, NX, NY, NZ), jnp.float32), -4.0, 4.0) * ramp
    return value.astype(jnp.float32)


def draw_solid_flag(key, part):
    rows = jnp.arange(NY, dtype=jnp.int32)
    threshold = 10 + 50 * rows // NY
    rolled = jax.random.randint(key, (NX, NY, NZ), 0, 100, dtype=jnp.int32)
    return (rolled < threshold[None, :, None]).astype(jnp.int32)


def draw_slot_counts(key, part):
    first, second, third = jax.random.split(jax.random.fold_in(key, 11), 3)
    factor = jax.random.randint(first, (DEVICES,), 1, 9, dtype=jnp.int32)
    bottom = CAP * factor // 16
    ceiling = CAP * factor // 8
    spread = jax.random.randint(second, (DEVICES, DEVICES), 0, 1 << 20, dtype=jnp.int32)
    counts = spread % (ceiling - bottom + 1)[None, :] + bottom[None, :]
    counts = jnp.maximum(counts, 1)
    full = jax.random.randint(third, (), 0, DEVICES, dtype=jnp.int32)
    counts = jnp.where(jnp.arange(DEVICES, dtype=jnp.int32)[None, :] == full, CAP, counts)
    return counts.astype(jnp.int32)


def draw_corner_base(key, part):
    first, second, third = jax.random.split(jax.random.fold_in(key, 23), 3)
    shape = (DEVICES, DEVICES, CAP)
    first_cell = jax.random.randint(first, shape, 0, CX - 1, dtype=jnp.int32)
    second_cell = jax.random.randint(second, shape, 0, CY - 1, dtype=jnp.int32)
    third_cell = jax.random.randint(third, shape, 0, CZ - 1, dtype=jnp.int32)
    flat = first_cell * (CY * CZ) + second_cell * CZ + third_cell
    flat = flat.at[0, 0, 0].set((CX - 2) * CY * CZ + (CY - 2) * CZ + CZ - 2)
    return flat.astype(jnp.int32)


def shard_levels(key, dims, cuts, smallest, high):
    factor_of, own = 1.0, jax.random.fold_in(key, 6)
    for dim, blocks in cuts:
        heights = jnp.exp(jax.random.uniform(jax.random.fold_in(own, dim), (blocks,), jnp.float32, smallest / len(cuts), high / len(cuts)))
        factor_of = factor_of * jnp.repeat(heights, dims[dim] // blocks).reshape([-1 if axis == dim else 1 for axis in range(len(dims))])
    return factor_of


def bell_draw(rng, dims, deviation, reach, shards=(), kind=jnp.bfloat16):
    drawn = deviation * jax.random.normal(rng, dims, jnp.float32)
    if shards:
        drawn = drawn * shard_levels(rng, dims, shards, -0.22, 0.18)
    return jnp.clip(drawn, -reach, reach).astype(kind)


def setup_inputs(seed: int = 0) -> dict:
    key_of = jax.random.split(jax.random.key(seed), 8)
    return {
        "part_mass": jnp.clip(jnp.exp(math.log(2.0) - 2.3025851 * jax.random.uniform(key_of[0], (DEVICES, DEVICES, CAP), jnp.float32) ** shard_levels(key_of[0], (DEVICES, DEVICES, CAP), ((0, 128),), -0.2, 0.2)), 0.2, 2.0),
        "part_vel": bell_draw(key_of[1], (DEVICES, DEVICES, 3, CAP), 1.0, 6.0, ((0, 128),), jnp.float32),
        "corner_weight": jnp.clip(0.25 * jax.random.uniform(key_of[2], (DEVICES, DEVICES, 8, CAP), jnp.float32) ** shard_levels(key_of[2], (DEVICES, DEVICES, 8, CAP), ((0, 128),), -0.2, 0.2), 0.0, 0.25),
        "corner_base": draw_corner_base(jax.random.fold_in(key_of[7], 71), 0),
        "slot_counts": draw_slot_counts(jax.random.fold_in(key_of[7], 71), 0),
        "water_vel": draw_water_vel(jax.random.fold_in(key_of[7], 71), 0),
        "solid_flag": draw_solid_flag(jax.random.fold_in(key_of[7], 71), 0),
    }


damping = 0.05
solid_water = 0.1
flip_ratio = 0.9
lower_bound = 0.1
upper_bound = 2.0


def harmonic(first, second):
    return 2.0 * first * second / (first + second)


def neighbours(padded):
    return [padded[2:, 1:-1, 1:-1], padded[:-2, 1:-1, 1:-1],
            padded[1:-1, 2:, 1:-1], padded[1:-1, :-2, 1:-1],
            padded[1:-1, 1:-1, 2:], padded[1:-1, 1:-1, :-2]]


def face_weights(kappa, padded):
    return [harmonic(kappa, other) for other in neighbours(padded)]


def diagonal_of(betas):
    result = damping
    for weight in betas:
        result = result + weight
    return result


def operate(field, padded, betas):
    result = damping * field
    for weight, other in zip(betas, neighbours(padded)):
        result = result + weight * (field - other)
    return result


def divergence(velocity, padded_list, betas):
    result = jnp.zeros_like(velocity[0])
    for axis_number in range(3):
        component = velocity[axis_number]
        near = neighbours(padded_list[axis_number])
        result = result + betas[2 * axis_number] * (component + near[2 * axis_number]) * 0.5
        result = result - betas[2 * axis_number + 1] * (near[2 * axis_number + 1] + component) * 0.5
    return result


def gradient(field, padded, betas):
    near = neighbours(padded)
    return [(betas[2 * axis_number] * (near[2 * axis_number] - field)
             + betas[2 * axis_number + 1] * (field - near[2 * axis_number + 1])) * 0.5
            for axis_number in range(3)]


def chebyshev(residual, inverse, apply):
    theta = (upper_bound + lower_bound) / 2.0
    delta = (upper_bound - lower_bound) / 2.0
    sigma = theta / delta
    update = inverse * residual / theta
    result = update
    previous = 1.0 / sigma
    for turn in range(DEGREE - 1):
        misfit = residual - apply(result)
        current = 1.0 / (2.0 * sigma - previous)
        update = current * previous * update + (2.0 * current / delta) * inverse * misfit
        result = result + update
        previous = current
    return result


def to_global(blocks, parts):
    shaped = blocks.reshape(N_GX, N_YZ, parts, CX, CY, CZ)
    return jnp.transpose(shaped, (2, 0, 3, 1, 4, 5)).reshape(parts, NX, NY, NZ)


def to_blocks(field, parts):
    shaped = field.reshape(parts, N_GX, CX, N_YZ, CY, CZ)
    return jnp.transpose(shaped, (1, 3, 0, 2, 4, 5)).reshape(DEVICES, parts, CX * CY * CZ)


def reference(part_mass, part_vel, corner_weight, corner_base, slot_counts, water_vel, solid_flag):
    cells = CX * CY * CZ
    offsets = jnp.array([((corner >> 2) & 1) * CY * CZ + ((corner >> 1) & 1) * CZ + (corner & 1)
                         for corner in range(8)], jnp.int32)
    live = (jnp.arange(CAP, dtype=jnp.int32)[None, None, :] < slot_counts[:, :, None]).astype(jnp.float32)

    def spread(target):
        masses = part_mass[:, target, :] * live[:, target, :]
        weighted = corner_weight[:, target] * masses[:, None, :]
        momentum = weighted[:, None] * part_vel[:, target][:, :, None]
        values = jnp.concatenate([weighted[:, None], momentum], axis=1)
        flat = jnp.transpose(values, (1, 0, 2, 3)).reshape(4, -1)
        places = (corner_base[:, target][:, None, :] + offsets[None, :, None]).reshape(-1)
        return jnp.zeros((4, cells), jnp.float32).at[:, places].add(flat)

    blocks = lax.map(spread, jnp.arange(DEVICES, dtype=jnp.int32))
    grid = to_global(blocks, 4)
    density = jnp.where(solid_flag == 1, solid_water, 1.0).astype(jnp.float32)
    total = grid[0] + density
    kappa = 1.0 / total
    velocity = (grid[1:] + density[None] * water_vel) / total[None]
    betas = face_weights(kappa, jnp.pad(kappa, 1))
    inverse = 1.0 / diagonal_of(betas)
    padded_velocity = [jnp.pad(velocity[axis_number], 1) for axis_number in range(3)]
    source = -divergence(velocity, padded_velocity, betas)

    def apply(field):
        return operate(field, jnp.pad(field, 1), betas)

    pressure = jnp.zeros_like(source)
    residual = source
    precond = chebyshev(residual, inverse, apply)
    search = precond
    agreement = jnp.sum(residual * precond)
    for turn in range(ITERS):
        image = apply(search)
        alpha = agreement / jnp.sum(search * image)
        pressure = pressure + alpha * search
        residual = residual - alpha * image
        if turn + 1 < ITERS:
            precond = chebyshev(residual, inverse, apply)
            agreement_next = jnp.sum(residual * precond)
            search = precond + (agreement_next / agreement) * search
            agreement = agreement_next
    slopes = gradient(pressure, jnp.pad(pressure, 1), betas)
    corrected = velocity - jnp.stack(slopes)
    carried = corrected - flip_ratio * velocity
    carried_blocks = to_blocks(carried, 3)

    def sample(target):
        places = corner_base[:, target][:, None, :] + offsets[None, :, None]
        picked = carried_blocks[target][:, places]
        return jnp.sum(picked * corner_weight[:, target][None], axis=2)

    sampled = lax.map(sample, jnp.arange(DEVICES, dtype=jnp.int32))
    sampled = jnp.transpose(sampled, (2, 0, 1, 3))
    return flip_ratio * part_vel + sampled, pressure
```

```python
import jax
import jax.numpy as jnp
from jax import lax
from jax.experimental import pallas as pl
from jax.experimental.pallas import tpu as pltpu
from jax.sharding import PartitionSpec as P

ALL = ("gx", "yz")
DAMPING = 0.05
SOLID_WATER = 0.1
FLIP = 0.9
LOWER = 0.1
UPPER = 2.0
DEGREE = 3
GROUPS = 128
CAP = 128
FIELDS = 13
ROW_W = 3
ROW_M = 11
ROW_B = 12
CELLS = 32
DEPTH = 512
CHUNK = 8
HALO = 4
YE = 8 + 2 * HALO
XE = 16
PARAMS = pltpu.CompilerParams(vmem_limit_bytes=60 * 1024 * 1024)
VM = pl.BlockSpec(memory_space=pltpu.VMEM)
SM = pl.BlockSpec(memory_space=pltpu.SMEM)
F32 = jnp.float32
BF16 = jnp.bfloat16


def shape(*dims):
    return jax.ShapeDtypeStruct(dims, F32)


def split(value):
    high = value.astype(BF16)
    return high, (value - high.astype(F32)).astype(BF16)


def cells_of(msg, plane_s, depth_s):
    base = msg[pl.ds(ROW_B, GROUPS, stride=FIELDS), :].astype(jnp.int32)
    plane = base >> 9
    plane_s[...] = (plane & 7) * 4 + (plane >> 3)
    depth_s[...] = base & 511


def tile_weights(msg, source, plane_row):
    away = lax.broadcasted_iota(jnp.int32, (CELLS, CAP), 0) - plane_row
    here, next_y, next_x, next_xy = away == 0, away == 4, away == 1, away == 5
    zero = jnp.zeros((CELLS, CAP), F32)

    def weight(corner):
        row = msg[pl.ds(FIELDS * source + ROW_W + corner, 1), :]
        return jnp.broadcast_to(row, (CELLS, CAP))

    lifts = []
    for lift in (0, 1):
        value = jnp.where(next_xy, weight(6 + lift), zero)
        value = jnp.where(next_x, weight(4 + lift), value)
        value = jnp.where(next_y, weight(2 + lift), value)
        lifts.append(jnp.where(here, weight(lift), value))
    return jnp.concatenate(lifts, axis=0)


def depth_hot(depth_row):
    level = lax.broadcasted_iota(jnp.int32, (DEPTH, CAP), 0)
    return jnp.where(level == depth_row, 1.0, 0.0).astype(BF16)


def spread_kernel(msg, density, water, out, plane_s, depth_s, value_s, left_a, hot_a, left_b, hot_b, acc):
    cells_of(msg, plane_s, depth_s)
    mass = msg[pl.ds(ROW_M, GROUPS, stride=FIELDS), :]
    value_s[0] = mass
    for axis in range(3):
        value_s[1 + axis] = mass * msg[pl.ds(axis, GROUPS, stride=FIELDS), :]
    acc[...] = jnp.zeros_like(acc)

    def build(chunk, left, hot):
        for j in range(CHUNK):
            source = chunk * CHUNK + j
            columns = slice(j * CAP, (j + 1) * CAP)
            weights = tile_weights(msg, source, plane_s[pl.ds(source, 1), :])
            for f in range(4):
                high, low = split(weights * value_s[f, pl.ds(source, 1), :])
                left[f * 64 : (f + 1) * 64, columns] = high
                left[256 + f * 64 : 256 + (f + 1) * 64, columns] = low
            hot[:, columns] = depth_hot(depth_s[pl.ds(source, 1), :])

    def multiply(left, hot):
        acc[...] += lax.dot_general(
            left[...], hot[...], (((1,), (1,)), ((), ())), preferred_element_type=F32
        )

    turns = GROUPS // CHUNK // 2
    build(0, left_a, hot_a)

    def body(turn, carry):
        build(2 * turn + 1, left_b, hot_b)
        multiply(left_a, hot_a)

        @pl.when(turn < turns - 1)
        def _():
            build(2 * turn + 2, left_a, hot_a)

        multiply(left_b, hot_b)
        return carry

    lax.fori_loop(0, turns, body, 0)
    grid = []
    for f in range(4):
        both = acc[f * 64 : (f + 1) * 64, :] + acc[256 + f * 64 : 256 + (f + 1) * 64, :]
        grid.append(both[:CELLS] + pltpu.roll(both[CELLS:], 1, 1))
    total = grid[0] + density[...]
    out[0] = total
    for axis in range(3):
        out[1 + axis] = (grid[1 + axis] + density[...] * water[axis]) / total


def spread(msg, density, water):
    operand = pltpu.VMEM((512, CHUNK * CAP), BF16)
    index = pltpu.VMEM((GROUPS, CAP), jnp.int32)
    return pl.pallas_call(
        spread_kernel,
        out_shape=shape(4, CELLS, DEPTH),
        in_specs=[VM] * 3,
        out_specs=VM,
        scratch_shapes=[index, index, pltpu.VMEM((4, GROUPS, CAP), F32)]
        + [operand] * 4
        + [pltpu.VMEM((512, DEPTH), F32)],
        compiler_params=PARAMS,
        name="spread",
    )(msg, density, water)


def next_x(row):
    return pltpu.roll(row, XE - 1, 0)


def prev_x(row):
    return pltpu.roll(row, 1, 0)


def next_z(row):
    return pltpu.roll(row, DEPTH - 1, 1)


def prev_z(row):
    return pltpu.roll(row, 1, 1)


def each_row(first, last, body):
    def step(y, carry):
        body(y)
        return carry

    lax.fori_loop(first, last, step, 0)


def operate_row(field, y, offset, beta_x, beta_y, beta_z):
    here = field[y - offset]
    flux_x = beta_x[y] * (here - next_x(here))
    flux_z = beta_z[y] * (here - next_z(here))
    flux_y = beta_y[y] * (here - field[y - offset + 1])
    from_y = beta_y[y - 1] * (field[y - offset - 1] - here)
    return (
        DAMPING * here
        + (flux_x - prev_x(flux_x))
        + (flux_y - from_y)
        + (flux_z - prev_z(flux_z))
    )


def place(ext, own, low_x, high_x, low_y, high_y, fix):
    for block, source in enumerate((low_x, own, high_x)):
        columns = slice(4 * block, 4 * block + 4)
        for y in range(8):
            ext[HALO + y, columns, :] = fix(source(slice(4 * y, 4 * y + 4)), block, 1)
        for y in range(HALO):
            rows = slice(4 * y, 4 * y + 4)
            ext[y, columns, :] = fix(low_y(block, rows), block, 0)
            ext[HALO + 8 + y, columns, :] = fix(high_y(block, rows), block, 2)


def precondition(residual, inverse, beta_x, beta_y, beta_z, update, first, second, finish):
    theta = (UPPER + LOWER) / 2.0
    delta = (UPPER - LOWER) / 2.0
    sigma = theta / delta

    def start(y):
        value = inverse[y] * residual[y] * (1.0 / theta)
        update[y] = value
        first[y] = value

    each_row(1, YE - 1, start)
    previous = 1.0 / sigma
    current = 1.0 / (2.0 * sigma - previous)

    def middle(y):
        misfit = residual[y] - operate_row(first, y, 0, beta_x, beta_y, beta_z)
        value = current * previous * update[y] + (2.0 * current / delta) * inverse[y] * misfit
        update[y] = value
        second[y] = first[y] + value

    each_row(2, YE - 2, middle)
    latest = 1.0 / (2.0 * sigma - current)

    def last(y):
        misfit = residual[y] - operate_row(second, y, 0, beta_x, beta_y, beta_z)
        value = latest * current * update[y] + (2.0 * latest / delta) * inverse[y] * misfit
        finish(y, second[y] + value)

    each_row(3, YE - 3, last)


def each_pair(body):
    def step(pair, carry):
        y = HALO + 2 * pair
        rows = pl.ds(pl.multiple_of(8 * pair, 8), 8)
        lower_half = lax.broadcasted_iota(jnp.int32, (8, DEPTH), 0) < 4
        for ref, first, second in zip(*body(y)):
            ref[rows, :] = jnp.where(lower_half, pltpu.roll(first[:8], 4, 0), second[:8])
        return carry

    lax.fori_loop(0, 4, step, 0)


def start_kernel(
    edge, own, low_x, high_x, low_y, high_y,
    beta_x, beta_y, beta_z, inverse, basis, basis_own, image, source_own,
    ext, residual, update, first, second,
):
    infinite = jnp.full((4, DEPTH), jnp.inf, F32)
    for f in range(4):
        ext[f, :, 12:16, :] = jnp.full((YE, 4, DEPTH), jnp.inf if f == 0 else 0.0, F32)

        def fix(value, block, row, f=f):
            if f or (block == 1 and row == 1):
                return value
            outside = 0
            if block != 1:
                outside = outside + edge[0 if block == 0 else 1]
            if row != 1:
                outside = outside + edge[2 if row == 0 else 3]
            return jnp.where(outside > 0, infinite, value)

        place(
            ext.at[f],
            lambda rows, f=f: own[f, rows, :],
            lambda rows, f=f: low_x[f, rows, :],
            lambda rows, f=f: high_x[f, rows, :],
            lambda block, rows, f=f: low_y[block, f, rows, :],
            lambda block, rows, f=f: high_y[block, f, rows, :],
            fix,
        )
    end = lax.broadcasted_iota(jnp.int32, (XE, DEPTH), 1) == DEPTH - 1

    def faces(y):
        total = ext[0, y]
        beta_x[y] = 2.0 / (total + next_x(total))
        beta_y[y] = 2.0 / (total + ext[0, y + 1])
        beta_z[y] = jnp.where(end, 0.0, 2.0 / (total + next_z(total)))

    each_row(0, YE - 1, faces)

    def source(y):
        across, along = beta_x[y], beta_z[y]
        diagonal = (
            DAMPING + across + prev_x(across) + beta_y[y] + beta_y[y - 1] + along + prev_z(along)
        )
        inverse[y] = 1.0 / diagonal
        vx, vy, vz = ext[1, y], ext[2, y], ext[3, y]
        flow_x = across * (vx + next_x(vx))
        flow_z = along * (vz + next_z(vz))
        flow_y = beta_y[y] * (vy + ext[2, y + 1]) - beta_y[y - 1] * (ext[2, y - 1] + vy)
        residual[y] = -0.5 * (
            (flow_x - prev_x(flow_x)) + flow_y + (flow_z - prev_z(flow_z))
        )

    each_row(1, YE - 1, source)

    def finish(y, value):
        basis[y - 3] = value

    precondition(residual, inverse, beta_x, beta_y, beta_z, update, first, second, finish)

    def apply(y):
        return operate_row(basis, y, 3, beta_x, beta_y, beta_z), basis[y - 3], residual[y]

    each_pair(lambda y: ((image, basis_own, source_own), apply(y), apply(y + 1)))


EXT = (YE, XE, DEPTH)
BASIS = (10, XE, DEPTH)
BLOCK = (CELLS, DEPTH)


def start_solve(edge, own, low_x, high_x, low_y, high_y):
    return pl.pallas_call(
        start_kernel,
        out_shape=[shape(*EXT)] * 4 + [shape(*BASIS)] + [shape(*BLOCK)] * 3,
        in_specs=[SM] + [VM] * 5,
        out_specs=[VM] * 8,
        scratch_shapes=[pltpu.VMEM((4,) + EXT, F32)] + [pltpu.VMEM(EXT, F32)] * 4,
        compiler_params=PARAMS,
        name="start_solve",
    )(edge, own, low_x, high_x, low_y, high_y)


def next_basis(own, low_x, high_x, low_y, high_y, betas, inverse, before, basis, basis_own, image, scratch):
    ext, update, first, second = scratch
    ext[:, 12:16, :] = jnp.zeros((YE, 4, DEPTH), F32)
    place(
        ext,
        lambda rows: own[rows, :],
        lambda rows: low_x[rows, :],
        lambda rows: high_x[rows, :],
        lambda block, rows: low_y[block, rows, :],
        lambda block, rows: high_y[block, rows, :],
        lambda value, block, row: value,
    )

    def finish(y, value):
        basis[y - 3] = before[y - 3] - value

    precondition(ext, inverse, *betas, update, first, second, finish)

    def apply(y):
        return operate_row(basis, y, 3, *betas), basis[y - 3]

    each_pair(lambda y: ((image, basis_own), apply(y), apply(y + 1)))


def middle_kernel(
    own, low_x, high_x, low_y, high_y, beta_x, beta_y, beta_z, inverse, before,
    basis, basis_own, image, *scratch,
):
    next_basis(
        own, low_x, high_x, low_y, high_y, (beta_x, beta_y, beta_z), inverse, before,
        basis, basis_own, image, scratch,
    )


def last_kernel(
    own, low_x, high_x, low_y, high_y, beta_x, beta_y, beta_z, inverse, before,
    own_0, own_1, image_0, source_own, basis, sums, own_2, image_2, *scratch,
):
    next_basis(
        own, low_x, high_x, low_y, high_y, (beta_x, beta_y, beta_z), inverse, before,
        basis, own_2, image_2, scratch,
    )
    vectors = (own_0[...], own_1[...], own_2[...])
    images = (image_0[...], own[...], image_2[...])
    source = source_own[...]
    pairs = [(vectors[i], images[j]) for i in range(3) for j in range(i, 3)]
    pairs += [(vector, source) for vector in vectors]
    lane = lax.broadcasted_iota(jnp.int32, (1, CAP), 1)
    row = jnp.zeros((1, CAP), F32)
    for place_in, (a, b) in enumerate(pairs):
        folded = jnp.sum((a * b).reshape(4, 8, DEPTH), axis=0)
        folded = (folded[:, :128] + folded[:, 128:256]) + (folded[:, 256:384] + folded[:, 384:])
        row = jnp.where(lane == place_in, jnp.sum(folded, keepdims=True), row)
    sums[...] = jnp.broadcast_to(row, (GROUPS, CAP))


def middle_solve(own, low_x, high_x, low_y, high_y, betas, inverse, before):
    return pl.pallas_call(
        middle_kernel,
        out_shape=[shape(*BASIS), shape(*BLOCK), shape(*BLOCK)],
        in_specs=[VM] * 10,
        out_specs=[VM] * 3,
        scratch_shapes=[pltpu.VMEM(EXT, F32)] * 4,
        compiler_params=PARAMS,
        name="middle_solve",
    )(own, low_x, high_x, low_y, high_y, *betas, inverse, before)


def last_solve(own, low_x, high_x, low_y, high_y, betas, inverse, before, *inner):
    return pl.pallas_call(
        last_kernel,
        out_shape=[shape(*BASIS), shape(GROUPS, CAP)],
        in_specs=[VM] * 14,
        out_specs=[VM] * 2,
        scratch_shapes=[pltpu.VMEM(BLOCK, F32)] * 2 + [pltpu.VMEM(EXT, F32)] * 4,
        compiler_params=PARAMS,
        name="last_solve",
    )(own, low_x, high_x, low_y, high_y, *betas, inverse, before, *inner)


def coefficients(sums):
    total = jnp.sum(sums[...], axis=0, keepdims=True)
    g00, g01, g02, g11, g12, g22, b0, b1, b2 = [total[:, k : k + 1] for k in range(9)]
    l1 = g01 / g00
    l2 = g02 / g00
    d1 = g11 - l1 * g01
    keep_1 = d1 > 1e-7 * g11
    d1 = jnp.where(keep_1, d1, 1.0)
    m = jnp.where(keep_1, (g12 - l2 * g01) / d1, 0.0)
    d2 = g22 - l2 * g02 - m * m * d1
    keep_2 = d2 > 1e-7 * g22
    d2 = jnp.where(keep_2, d2, 1.0)
    y1 = b1 - l1 * b0
    y2 = b2 - l2 * b0 - m * y1
    c2 = jnp.where(keep_2, y2 / d2, 0.0)
    c1 = jnp.where(keep_1, y1 / d1, 0.0) - m * c2
    c0 = b0 / g00 - l1 * c1 - l2 * c2
    return c0, c1, c2


def gather_kernel(
    sums, basis_0, basis_1, basis_2, beta_x, beta_y, beta_z, own, msg,
    out, pressure_out, plane_s, depth_s, pressure, carried, high_s, low_s,
):
    c0, c1, c2 = [jnp.broadcast_to(c, (XE, DEPTH)) for c in coefficients(sums)]

    def combine(y):
        pressure[y] = c0 * basis_0[y] + c1 * basis_1[y] + c2 * basis_2[y]

    each_row(0, 10, combine)

    def slopes(y):
        here = pressure[y - 3]
        flux_x = beta_x[y] * (here - next_x(here))
        flux_z = beta_z[y] * (here - next_z(here))
        flux_y = beta_y[y] * (here - pressure[y - 2])
        from_y = beta_y[y - 1] * (pressure[y - 4] - here)
        return (
            (flux_x + prev_x(flux_x)) * 0.5,
            (flux_y + from_y) * 0.5,
            (flux_z + prev_z(flux_z)) * 0.5,
            here,
        )

    targets = (carried.at[0], carried.at[1], carried.at[2], pressure_out)
    each_pair(lambda y: (targets, slopes(y), slopes(y + 1)))
    for axis in range(3):
        velocity = own[1 + axis]
        value = (velocity + carried[axis]) - FLIP * velocity
        for lift, level in ((0, value), (1, next_z(value))):
            high, low = split(level)
            rows = slice(axis * 64 + lift * CELLS, axis * 64 + (lift + 1) * CELLS)
            high_s[rows, :] = high
            low_s[rows, :] = low
    cells_of(msg, plane_s, depth_s)

    def body(chunk, carry):
        hots = [depth_hot(depth_s[pl.ds(chunk * CHUNK + j, 1), :]) for j in range(CHUNK)]
        hot = jnp.concatenate(hots, axis=1)
        table = jnp.dot(high_s[...], hot, preferred_element_type=F32)
        table = table + jnp.dot(low_s[...], hot, preferred_element_type=F32)
        for j in range(CHUNK):
            source = chunk * CHUNK + j
            weights = tile_weights(msg, source, plane_s[pl.ds(source, 1), :])
            for axis in range(3):
                picked = table[axis * 64 : (axis + 1) * 64, j * CAP : (j + 1) * CAP] * weights
                out[pl.ds(3 * source + axis, 1), :] = jnp.sum(picked, axis=0, keepdims=True)
        return carry

    lax.fori_loop(0, GROUPS // CHUNK, body, 0)


def gather(sums, bases, betas, own, msg):
    index = pltpu.VMEM((GROUPS, CAP), jnp.int32)
    operand = pltpu.VMEM((192, DEPTH), BF16)
    return pl.pallas_call(
        gather_kernel,
        out_shape=[shape(3 * GROUPS, CAP), shape(*BLOCK)],
        in_specs=[VM] * 9,
        out_specs=[VM] * 2,
        scratch_shapes=[index, index, pltpu.VMEM(BASIS, F32), pltpu.VMEM((3,) + BLOCK, F32), operand, operand],
        compiler_params=PARAMS,
        name="gather",
    )(sums, *bases, *betas, own, msg)


def exchange(block, n_x, n_y):
    up_x = [(i, (i + 1) % n_x) for i in range(n_x)]
    up_y = [(i, (i + 1) % n_y) for i in range(n_y)]
    low_x = lax.ppermute(block, "gx", up_x)
    high_x = lax.ppermute(block, "gx", [(b, a) for a, b in up_x])
    half = CELLS // 2
    upper = jnp.stack([b[..., half:, :] for b in (low_x, block, high_x)])
    lower = jnp.stack([b[..., :half, :] for b in (low_x, block, high_x)])
    low_y = lax.ppermute(upper, "yz", up_y)
    high_y = lax.ppermute(lower, "yz", [(b, a) for a, b in up_y])
    return low_x, high_x, low_y, high_y


def by_block(field):
    turned = jnp.swapaxes(field, -3, -2)
    return turned.reshape(turned.shape[:-3] + (CELLS, DEPTH))


def local(part_mass, part_vel, corner_weight, corner_base, slot_counts, water_vel, solid_flag):
    n_x, n_y = lax.axis_size("gx"), lax.axis_size("yz")
    at_x, at_y = lax.axis_index("gx"), lax.axis_index("yz")
    edge = jnp.stack([at_x == 0, at_x == n_x - 1, at_y == 0, at_y == n_y - 1]).astype(jnp.int32)
    slot = jnp.arange(CAP, dtype=jnp.int32)
    live = (slot[None, :] < slot_counts[0][:, None]).astype(F32)
    masses = part_mass[0] * live
    message = jnp.concatenate(
        [part_vel[0], corner_weight[0], masses[:, None], corner_base[0].astype(F32)[:, None]], axis=1
    )
    msg = lax.all_to_all(message.reshape(GROUPS, FIELDS * CAP), ALL, 0, 0, tiled=True)
    msg = msg.reshape(GROUPS * FIELDS, CAP)
    density = by_block(jnp.where(solid_flag == 1, SOLID_WATER, 1.0).astype(F32))
    own = spread(msg, density, by_block(water_vel))
    *rest, basis_0, own_0, image_0, source = start_solve(edge, own, *exchange(own, n_x, n_y))
    betas, inverse = rest[:3], rest[3]
    basis_1, own_1, image_1 = middle_solve(image_0, *exchange(image_0, n_x, n_y), betas, inverse, basis_0)
    basis_2, sums = last_solve(
        image_1, *exchange(image_1, n_x, n_y), betas, inverse, basis_1, own_0, own_1, image_0, source
    )
    sums = lax.all_to_all(sums, ALL, 0, 0, tiled=True)
    sampled, pressure = gather(sums, (basis_0, basis_1, basis_2), betas, own, msg)
    returned = lax.all_to_all(sampled.reshape(GROUPS, 3 * CAP), ALL, 0, 0, tiled=True)
    returned = returned.reshape(1, GROUPS, 3, CAP)
    pressure = jnp.swapaxes(pressure.reshape(8, 4, DEPTH), 0, 1)
    return FLIP * part_vel + returned, pressure


def solution(mesh):
    parts = P(ALL, None, None)
    in_specs = (parts, P(ALL, None, None, None), P(ALL, None, None, None), parts, P(ALL, None), P(None, "gx", "yz", None), P("gx", "yz", None))
    out_specs = (P(ALL, None, None, None), P("gx", "yz", None))
    return jax.shard_map(local, mesh=mesh, in_specs=in_specs, out_specs=out_specs, check_vma=False)
```

```python
import jax
import jax.numpy as jnp
from jax import lax
from jax.experimental import pallas as pl
from jax.experimental.pallas import tpu as pltpu
from jax.sharding import PartitionSpec as P

ALL = ("gx", "yz")
DAMPING = 0.05
SOLID_WATER = 0.1
FLIP = 0.9
LOWER = 0.1
UPPER = 2.0
DEGREE = 3
GROUPS = 128
CAP = 128
FIELDS = 13
ROW_W = 3
ROW_M = 11
ROW_B = 12
CELLS = 32
DEPTH = 512
CHUNK = 8
HALO = 4
YE = 8 + 2 * HALO
XE = 16
PARAMS = pltpu.CompilerParams(vmem_limit_bytes=20 * 1024 * 1024)
VM = pl.BlockSpec(memory_space=pltpu.VMEM)
SM = pl.BlockSpec(memory_space=pltpu.SMEM)
F32 = jnp.float32
BF16 = jnp.bfloat16


def shape(*dims):
    return jax.ShapeDtypeStruct(dims, F32)


def remainder(value):
    return value - value.astype(BF16).astype(F32)


def one_pass(left, right):
    return lax.dot_general(
        left, right, (((1,), (0,)), ((), ())), precision=lax.Precision.DEFAULT, preferred_element_type=F32
    )


def cells_of(msg, plane_s, depth_s):
    base = msg[pl.ds(ROW_B, GROUPS, stride=FIELDS), :].astype(jnp.int32)
    plane = base >> 9
    plane_s[...] = (plane & 7) * 4 + (plane >> 3)
    depth_s[...] = base & 511


def tile_weights(msg, source, plane_row):
    away = lax.broadcasted_iota(jnp.int32, (CELLS, CAP), 0) - plane_row
    here, next_y, next_x, next_xy = away == 0, away == 4, away == 1, away == 5
    zero = jnp.zeros((CELLS, CAP), F32)

    def weight(corner):
        row = msg[pl.ds(FIELDS * source + ROW_W + corner, 1), :]
        return jnp.broadcast_to(row, (CELLS, CAP))

    lifts = []
    for lift in (0, 1):
        value = jnp.where(next_xy, weight(6 + lift), zero)
        value = jnp.where(next_x, weight(4 + lift), value)
        value = jnp.where(next_y, weight(2 + lift), value)
        lifts.append(jnp.where(here, weight(lift), value))
    return jnp.concatenate(lifts, axis=0)


def spread_kernel(msg, density, water, out, plane_s, depth_s, value_s, left_a, hot_a, left_b, hot_b, acc):
    cells_of(msg, plane_s, depth_s)
    depth_s[...] = depth_s[...].astype(F32).T.astype(jnp.int32)
    mass = msg[pl.ds(ROW_M, GROUPS, stride=FIELDS), :]
    value_s[0] = mass
    for axis in range(3):
        value_s[1 + axis] = mass * msg[pl.ds(axis, GROUPS, stride=FIELDS), :]
    acc[...] = jnp.zeros_like(acc)
    level = lax.broadcasted_iota(jnp.int32, (CAP, DEPTH), 1)

    def build(chunk, left, hot):
        depths = pltpu.roll(depth_s[...], (GROUPS - chunk * CHUNK) % GROUPS, 1)
        for j in range(CHUNK):
            source = chunk * CHUNK + j
            columns = slice(j * CAP, (j + 1) * CAP)
            weights = tile_weights(msg, source, plane_s[pl.ds(source, 1), :])
            for f in range(4):
                value = weights * value_s[f, pl.ds(source, 1), :]
                left[f * 64 : (f + 1) * 64, columns] = value
                left[256 + f * 64 : 256 + (f + 1) * 64, columns] = remainder(value)
            hot[columns, :] = jnp.where(level == depths[:, j : j + 1], 1.0, 0.0)

    def multiply(left, hot):
        acc[...] += one_pass(left[...], hot[...])

    turns = GROUPS // CHUNK
    build(0, left_a, hot_a)

    def body(turn, carry):
        build(2 * turn + 1, left_b, hot_b)
        multiply(left_a, hot_a)
        build((2 * turn + 2) & (turns - 1), left_a, hot_a)
        multiply(left_b, hot_b)
        return carry

    lax.fori_loop(0, turns // 2, body, 0)
    grid = []
    for f in range(4):
        both = acc[f * 64 : (f + 1) * 64, :] + acc[256 + f * 64 : 256 + (f + 1) * 64, :]
        grid.append(both[:CELLS] + pltpu.roll(both[CELLS:], 1, 1))
    total = grid[0] + density[...]
    out[0] = total
    for axis in range(3):
        out[1 + axis] = (grid[1 + axis] + density[...] * water[axis]) / total


def spread(msg, density, water):
    left = pltpu.VMEM((512, CHUNK * CAP), F32)
    hot = pltpu.VMEM((CHUNK * CAP, DEPTH), F32)
    index = pltpu.VMEM((GROUPS, CAP), jnp.int32)
    return pl.pallas_call(
        spread_kernel,
        out_shape=shape(4, CELLS, DEPTH),
        in_specs=[VM] * 3,
        out_specs=VM,
        scratch_shapes=[index, index, pltpu.VMEM((4, GROUPS, CAP), F32)]
        + [left, hot, left, hot]
        + [pltpu.VMEM((512, DEPTH), F32)],
        compiler_params=PARAMS,
        name="spread",
    )(msg, density, water)


def next_x(row):
    return pltpu.roll(row, XE - 1, 0)


def prev_x(row):
    return pltpu.roll(row, 1, 0)


def next_z(row):
    return pltpu.roll(row, DEPTH - 1, 1)


def prev_z(row):
    return pltpu.roll(row, 1, 1)


def each_row(first, last, body):
    def step(y, carry):
        body(y)
        return carry

    lax.fori_loop(first, last, step, 0)


def operate_row(field, y, offset, beta_x, beta_y, beta_z):
    here = field[y - offset]
    flux_x = beta_x[y] * (here - next_x(here))
    flux_z = beta_z[y] * (here - next_z(here))
    flux_y = beta_y[y] * (here - field[y - offset + 1])
    from_y = beta_y[y - 1] * (field[y - offset - 1] - here)
    return (
        DAMPING * here
        + (flux_x - prev_x(flux_x))
        + (flux_y - from_y)
        + (flux_z - prev_z(flux_z))
    )


def place(ext, own, low_x, high_x, low_y, high_y, fix):
    for block, source in enumerate((low_x, own, high_x)):
        columns = slice(4 * block, 4 * block + 4)
        for y in range(8):
            ext[HALO + y, columns, :] = fix(source(slice(4 * y, 4 * y + 4)), block, 1)
        for y in range(HALO):
            rows = slice(4 * y, 4 * y + 4)
            ext[y, columns, :] = fix(low_y(block, rows), block, 0)
            ext[HALO + 8 + y, columns, :] = fix(high_y(block, rows), block, 2)


def precondition(residual, inverse, beta_x, beta_y, beta_z, update, first, second, finish):
    theta = (UPPER + LOWER) / 2.0
    delta = (UPPER - LOWER) / 2.0
    sigma = theta / delta

    def start(y):
        value = inverse[y] * residual[y] * (1.0 / theta)
        update[y] = value
        first[y] = value

    each_row(1, YE - 1, start)
    previous = 1.0 / sigma
    current = 1.0 / (2.0 * sigma - previous)

    def middle(y):
        misfit = residual[y] - operate_row(first, y, 0, beta_x, beta_y, beta_z)
        value = current * previous * update[y] + (2.0 * current / delta) * inverse[y] * misfit
        update[y] = value
        second[y] = first[y] + value

    each_row(2, YE - 2, middle)
    latest = 1.0 / (2.0 * sigma - current)

    def last(y):
        misfit = residual[y] - operate_row(second, y, 0, beta_x, beta_y, beta_z)
        value = latest * current * update[y] + (2.0 * latest / delta) * inverse[y] * misfit
        finish(y, second[y] + value)

    each_row(3, YE - 3, last)


def each_pair(body):
    def step(pair, carry):
        y = HALO + 2 * pair
        rows = pl.ds(pl.multiple_of(8 * pair, 8), 8)
        lower_half = lax.broadcasted_iota(jnp.int32, (8, DEPTH), 0) < 4
        for ref, first, second in zip(*body(y)):
            ref[rows, :] = jnp.where(lower_half, pltpu.roll(first[:8], 4, 0), second[:8])
        return carry

    lax.fori_loop(0, 4, step, 0)


def start_kernel(
    edge, own, low_x, high_x, low_y, high_y,
    beta_x, beta_y, beta_z, inverse, basis, basis_own, image, source_own,
    ext, residual, update, first, second,
):
    infinite = jnp.full((4, DEPTH), jnp.inf, F32)
    for f in range(4):
        ext[f, :, 12:16, :] = jnp.full((YE, 4, DEPTH), jnp.inf if f == 0 else 0.0, F32)

        def fix(value, block, row, f=f):
            if f or (block == 1 and row == 1):
                return value
            outside = 0
            if block != 1:
                outside = outside + edge[0 if block == 0 else 1]
            if row != 1:
                outside = outside + edge[2 if row == 0 else 3]
            return jnp.where(outside > 0, infinite, value)

        place(
            ext.at[f],
            lambda rows, f=f: own[f, rows, :],
            lambda rows, f=f: low_x[f, rows, :],
            lambda rows, f=f: high_x[f, rows, :],
            lambda block, rows, f=f: low_y[block, f, rows, :],
            lambda block, rows, f=f: high_y[block, f, rows, :],
            fix,
        )
    end = lax.broadcasted_iota(jnp.int32, (XE, DEPTH), 1) == DEPTH - 1

    def faces(y):
        total = ext[0, y]
        beta_x[y] = 2.0 / (total + next_x(total))
        beta_y[y] = 2.0 / (total + ext[0, y + 1])
        beta_z[y] = jnp.where(end, 0.0, 2.0 / (total + next_z(total)))

    each_row(0, YE - 1, faces)

    def source(y):
        across, along = beta_x[y], beta_z[y]
        diagonal = (
            DAMPING + across + prev_x(across) + beta_y[y] + beta_y[y - 1] + along + prev_z(along)
        )
        inverse[y] = 1.0 / diagonal
        vx, vy, vz = ext[1, y], ext[2, y], ext[3, y]
        flow_x = across * (vx + next_x(vx))
        flow_z = along * (vz + next_z(vz))
        flow_y = beta_y[y] * (vy + ext[2, y + 1]) - beta_y[y - 1] * (ext[2, y - 1] + vy)
        residual[y] = -0.5 * (
            (flow_x - prev_x(flow_x)) + flow_y + (flow_z - prev_z(flow_z))
        )

    each_row(1, YE - 1, source)

    def finish(y, value):
        basis[y - 3] = value

    precondition(residual, inverse, beta_x, beta_y, beta_z, update, first, second, finish)

    def apply(y):
        return operate_row(basis, y, 3, beta_x, beta_y, beta_z), basis[y - 3], residual[y]

    each_pair(lambda y: ((image, basis_own, source_own), apply(y), apply(y + 1)))


EXT = (YE, XE, DEPTH)
BASIS = (10, XE, DEPTH)
BLOCK = (CELLS, DEPTH)


def start_solve(edge, own, low_x, high_x, low_y, high_y):
    return pl.pallas_call(
        start_kernel,
        out_shape=[shape(*EXT)] * 4 + [shape(*BASIS)] + [shape(*BLOCK)] * 3,
        in_specs=[SM] + [VM] * 5,
        out_specs=[VM] * 8,
        scratch_shapes=[pltpu.VMEM((4,) + EXT, F32)] + [pltpu.VMEM(EXT, F32)] * 4,
        compiler_params=PARAMS,
        name="start_solve",
    )(edge, own, low_x, high_x, low_y, high_y)


def next_basis(own, low_x, high_x, low_y, high_y, betas, inverse, before, basis, basis_own, image, scratch):
    ext, update, first, second = scratch
    ext[:, 12:16, :] = jnp.zeros((YE, 4, DEPTH), F32)
    place(
        ext,
        lambda rows: own[rows, :],
        lambda rows: low_x[rows, :],
        lambda rows: high_x[rows, :],
        lambda block, rows: low_y[block, rows, :],
        lambda block, rows: high_y[block, rows, :],
        lambda value, block, row: value,
    )

    def finish(y, value):
        basis[y - 3] = before[y - 3] - value

    precondition(ext, inverse, *betas, update, first, second, finish)

    def apply(y):
        return operate_row(basis, y, 3, *betas), basis[y - 3]

    each_pair(lambda y: ((image, basis_own), apply(y), apply(y + 1)))


def middle_kernel(
    own, low_x, high_x, low_y, high_y, beta_x, beta_y, beta_z, inverse, before,
    basis, basis_own, image, *scratch,
):
    next_basis(
        own, low_x, high_x, low_y, high_y, (beta_x, beta_y, beta_z), inverse, before,
        basis, basis_own, image, scratch,
    )


def last_kernel(
    own, low_x, high_x, low_y, high_y, beta_x, beta_y, beta_z, inverse, before,
    own_0, own_1, image_0, source_own, basis, sums, own_2, image_2, *scratch,
):
    next_basis(
        own, low_x, high_x, low_y, high_y, (beta_x, beta_y, beta_z), inverse, before,
        basis, own_2, image_2, scratch,
    )
    vectors = (own_0[...], own_1[...], own_2[...])
    images = (image_0[...], own[...], image_2[...])
    source = source_own[...]
    pairs = [(vectors[i], images[j]) for i in range(3) for j in range(i, 3)]
    pairs += [(vector, source) for vector in vectors]
    lane = lax.broadcasted_iota(jnp.int32, (1, CAP), 1)
    row = jnp.zeros((1, CAP), F32)
    for place_in, (a, b) in enumerate(pairs):
        folded = jnp.sum((a * b).reshape(4, 8, DEPTH), axis=0)
        folded = (folded[:, :128] + folded[:, 128:256]) + (folded[:, 256:384] + folded[:, 384:])
        row = jnp.where(lane == place_in, jnp.sum(folded, keepdims=True), row)
    sums[...] = jnp.broadcast_to(row, (GROUPS, CAP))


def middle_solve(own, low_x, high_x, low_y, high_y, betas, inverse, before):
    return pl.pallas_call(
        middle_kernel,
        out_shape=[shape(*BASIS), shape(*BLOCK), shape(*BLOCK)],
        in_specs=[VM] * 10,
        out_specs=[VM] * 3,
        scratch_shapes=[pltpu.VMEM(EXT, F32)] * 4,
        compiler_params=PARAMS,
        name="middle_solve",
    )(own, low_x, high_x, low_y, high_y, *betas, inverse, before)


def last_solve(own, low_x, high_x, low_y, high_y, betas, inverse, before, *inner):
    return pl.pallas_call(
        last_kernel,
        out_shape=[shape(*BASIS), shape(GROUPS, CAP)],
        in_specs=[VM] * 14,
        out_specs=[VM] * 2,
        scratch_shapes=[pltpu.VMEM(BLOCK, F32)] * 2 + [pltpu.VMEM(EXT, F32)] * 4,
        compiler_params=PARAMS,
        name="last_solve",
    )(own, low_x, high_x, low_y, high_y, *betas, inverse, before, *inner)


def coefficients(sums):
    total = jnp.sum(sums[...], axis=0, keepdims=True)
    g00, g01, g02, g11, g12, g22, b0, b1, b2 = [total[:, k : k + 1] for k in range(9)]
    l1 = g01 / g00
    l2 = g02 / g00
    d1 = g11 - l1 * g01
    keep_1 = d1 > 1e-7 * g11
    d1 = jnp.where(keep_1, d1, 1.0)
    m = jnp.where(keep_1, (g12 - l2 * g01) / d1, 0.0)
    d2 = g22 - l2 * g02 - m * m * d1
    keep_2 = d2 > 1e-7 * g22
    d2 = jnp.where(keep_2, d2, 1.0)
    y1 = b1 - l1 * b0
    y2 = b2 - l2 * b0 - m * y1
    c2 = jnp.where(keep_2, y2 / d2, 0.0)
    c1 = jnp.where(keep_1, y1 / d1, 0.0) - m * c2
    c0 = b0 / g00 - l1 * c1 - l2 * c2
    return c0, c1, c2


def gather_kernel(
    sums, basis_0, basis_1, basis_2, beta_x, beta_y, beta_z, own, msg,
    out, pressure_out, plane_s, depth_s, pressure, carried, table_s, hot_a, hot_b,
):
    c0, c1, c2 = [jnp.broadcast_to(c, (XE, DEPTH)) for c in coefficients(sums)]

    def combine(y):
        pressure[y] = c0 * basis_0[y] + c1 * basis_1[y] + c2 * basis_2[y]

    each_row(0, 10, combine)

    def slopes(y):
        here = pressure[y - 3]
        flux_x = beta_x[y] * (here - next_x(here))
        flux_z = beta_z[y] * (here - next_z(here))
        flux_y = beta_y[y] * (here - pressure[y - 2])
        from_y = beta_y[y - 1] * (pressure[y - 4] - here)
        return (
            (flux_x + prev_x(flux_x)) * 0.5,
            (flux_y + from_y) * 0.5,
            (flux_z + prev_z(flux_z)) * 0.5,
            here,
        )

    targets = (carried.at[0], carried.at[1], carried.at[2], pressure_out)
    each_pair(lambda y: (targets, slopes(y), slopes(y + 1)))
    for axis in range(3):
        velocity = own[1 + axis]
        value = (velocity + carried[axis]) - FLIP * velocity
        for lift, level in ((0, value), (1, next_z(value))):
            first = axis * 64 + lift * CELLS
            table_s[first : first + CELLS, :] = level
            table_s[192 + first : 192 + first + CELLS, :] = remainder(level)
    cells_of(msg, plane_s, depth_s)
    level = lax.broadcasted_iota(jnp.int32, (DEPTH, CAP), 0)

    def build(chunk, hot):
        for j in range(CHUNK):
            depth_row = depth_s[pl.ds(chunk * CHUNK + j, 1), :]
            hot[:, j * CAP : (j + 1) * CAP] = jnp.where(level == depth_row, 1.0, 0.0)

    def pick(chunk, hot):
        both = one_pass(table_s[...], hot[...])
        table = both[:192] + both[192:]
        for j in range(CHUNK):
            source = chunk * CHUNK + j
            weights = tile_weights(msg, source, plane_s[pl.ds(source, 1), :])
            for axis in range(3):
                picked = table[axis * 64 : (axis + 1) * 64, j * CAP : (j + 1) * CAP] * weights
                out[pl.ds(3 * source + axis, 1), :] = jnp.sum(picked, axis=0, keepdims=True)

    turns = GROUPS // CHUNK
    build(0, hot_a)

    def body(turn, carry):
        build(2 * turn + 1, hot_b)
        pick(2 * turn, hot_a)
        build((2 * turn + 2) & (turns - 1), hot_a)
        pick(2 * turn + 1, hot_b)
        return carry

    lax.fori_loop(0, turns // 2, body, 0)


def gather(sums, bases, betas, own, msg):
    index = pltpu.VMEM((GROUPS, CAP), jnp.int32)
    hot = pltpu.VMEM((DEPTH, CHUNK * CAP), F32)
    return pl.pallas_call(
        gather_kernel,
        out_shape=[shape(3 * GROUPS, CAP), shape(*BLOCK)],
        in_specs=[VM] * 9,
        out_specs=[VM] * 2,
        scratch_shapes=[index, index, pltpu.VMEM(BASIS, F32), pltpu.VMEM((3,) + BLOCK, F32), pltpu.VMEM((384, DEPTH), F32), hot, hot],
        compiler_params=PARAMS,
        name="gather",
    )(sums, *bases, *betas, own, msg)


def exchange(block, n_x, n_y):
    up_x = [(i, (i + 1) % n_x) for i in range(n_x)]
    up_y = [(i, (i + 1) % n_y) for i in range(n_y)]
    low_x = lax.ppermute(block, "gx", up_x)
    high_x = lax.ppermute(block, "gx", [(b, a) for a, b in up_x])
    half = CELLS // 2
    upper = jnp.stack([b[..., half:, :] for b in (low_x, block, high_x)])
    lower = jnp.stack([b[..., :half, :] for b in (low_x, block, high_x)])
    low_y = lax.ppermute(upper, "yz", up_y)
    high_y = lax.ppermute(lower, "yz", [(b, a) for a, b in up_y])
    return low_x, high_x, low_y, high_y


def by_block(field):
    turned = jnp.swapaxes(field, -3, -2)
    return turned.reshape(turned.shape[:-3] + (CELLS, DEPTH))


def local(part_mass, part_vel, corner_weight, corner_base, slot_counts, water_vel, solid_flag):
    n_x, n_y = lax.axis_size("gx"), lax.axis_size("yz")
    at_x, at_y = lax.axis_index("gx"), lax.axis_index("yz")
    edge = jnp.stack([at_x == 0, at_x == n_x - 1, at_y == 0, at_y == n_y - 1]).astype(jnp.int32)
    slot = jnp.arange(CAP, dtype=jnp.int32)
    live = (slot[None, :] < slot_counts[0][:, None]).astype(F32)
    masses = part_mass[0] * live
    message = jnp.concatenate(
        [part_vel[0], corner_weight[0], masses[:, None], corner_base[0].astype(F32)[:, None]], axis=1
    )
    msg = lax.all_to_all(message.reshape(GROUPS, FIELDS * CAP), ALL, 0, 0, tiled=True)
    msg = msg.reshape(GROUPS * FIELDS, CAP)
    density = by_block(jnp.where(solid_flag == 1, SOLID_WATER, 1.0).astype(F32))
    own = spread(msg, density, by_block(water_vel))
    *rest, basis_0, own_0, image_0, source = start_solve(edge, own, *exchange(own, n_x, n_y))
    betas, inverse = rest[:3], rest[3]
    basis_1, own_1, image_1 = middle_solve(image_0, *exchange(image_0, n_x, n_y), betas, inverse, basis_0)
    basis_2, sums = last_solve(
        image_1, *exchange(image_1, n_x, n_y), betas, inverse, basis_1, own_0, own_1, image_0, source
    )
    sums = lax.all_to_all(sums, ALL, 0, 0, tiled=True)
    sampled, pressure = gather(sums, (basis_0, basis_1, basis_2), betas, own, msg)
    returned = lax.all_to_all(sampled.reshape(GROUPS, 3 * CAP), ALL, 0, 0, tiled=True)
    returned = returned.reshape(1, GROUPS, 3, CAP)
    pressure = jnp.swapaxes(pressure.reshape(8, 4, DEPTH), 0, 1)
    return FLIP * part_vel + returned, pressure


def solution(mesh):
    parts = P(ALL, None, None)
    in_specs = (parts, P(ALL, None, None, None), P(ALL, None, None, None), parts, P(ALL, None), P(None, "gx", "yz", None), P("gx", "yz", None))
    out_specs = (P(ALL, None, None, None), P("gx", "yz", None))
    return jax.shard_map(local, mesh=mesh, in_specs=in_specs, out_specs=out_specs, check_vma=False)
```

```python
import jax
import jax.numpy as jnp
from jax import lax
from jax.experimental import pallas as pl
from jax.experimental.pallas import tpu as pltpu
from jax.sharding import PartitionSpec as P

ALL = ("gx", "yz")
DAMPING = 0.05
SOLID_WATER = 0.1
FLIP = 0.9
LOWER = 0.1
UPPER = 2.0
DEGREE = 3
GROUPS = 128
CAP = 128
FIELDS = 13
ROW_W = 3
ROW_M = 11
ROW_B = 12
CELLS = 32
DEPTH = 512
CHUNK = 8
HALO = 4
CORNER = 3
YE = 8 + 2 * HALO
XE = 16
PARAMS = pltpu.CompilerParams(vmem_limit_bytes=20 * 1024 * 1024)
SMALL = pltpu.CompilerParams(vmem_limit_bytes=8 * 1024 * 1024)
VM = pl.BlockSpec(memory_space=pltpu.VMEM)
SM = pl.BlockSpec(memory_space=pltpu.SMEM)
F32 = jnp.float32
BF16 = jnp.bfloat16


def shape(*dims):
    return jax.ShapeDtypeStruct(dims, F32)


def remainder(value):
    return value - value.astype(BF16).astype(F32)


def one_pass(left, right):
    return lax.dot_general(
        left, right, (((1,), (0,)), ((), ())), precision=lax.Precision.DEFAULT, preferred_element_type=F32
    )


def cells_of(msg, plane_s, depth_s):
    base = msg[pl.ds(ROW_B, GROUPS, stride=FIELDS), :].astype(jnp.int32)
    plane = base >> 9
    plane_s[...] = (plane & 7) * 4 + (plane >> 3)
    depth_s[...] = base & 511


def tile_weights(msg, source, plane_row):
    away = lax.broadcasted_iota(jnp.int32, (CELLS, CAP), 0) - plane_row
    here, next_y, next_x, next_xy = away == 0, away == 4, away == 1, away == 5
    zero = jnp.zeros((CELLS, CAP), F32)

    def weight(corner):
        row = msg[pl.ds(FIELDS * source + ROW_W + corner, 1), :]
        return jnp.broadcast_to(row, (CELLS, CAP))

    lifts = []
    for lift in (0, 1):
        value = jnp.where(next_xy, weight(6 + lift), zero)
        value = jnp.where(next_x, weight(4 + lift), value)
        value = jnp.where(next_y, weight(2 + lift), value)
        lifts.append(jnp.where(here, weight(lift), value))
    return jnp.concatenate(lifts, axis=0)


def pack_kernel(mass_h, velocity_h, weight_h, base_h, count_h, out, mass, velocity, weight, base, count, sems):
    pairs = ((count_h, count), (mass_h, mass), (base_h, base), (velocity_h, velocity), (weight_h, weight))
    copies = [pltpu.make_async_copy(a, b, sems.at[k]) for k, (a, b) in enumerate(pairs)]
    for copy in copies:
        copy.start()
    copies[0].wait()
    limit = jnp.broadcast_to(count[...], (GROUPS, CAP)).astype(F32).T
    slot = lax.broadcasted_iota(jnp.int32, (GROUPS, CAP), 1).astype(F32)
    live = jnp.where(slot < limit, 1.0, 0.0)
    copies[1].wait()
    out[pl.ds(ROW_M, GROUPS, stride=FIELDS), :] = mass[...] * live
    copies[2].wait()
    out[pl.ds(ROW_B, GROUPS, stride=FIELDS), :] = base[...].astype(F32)
    copies[3].wait()
    for axis in range(3):
        out[pl.ds(axis, GROUPS, stride=FIELDS), :] = velocity[axis]
    copies[4].wait()
    for corner in range(8):
        out[pl.ds(ROW_W + corner, GROUPS, stride=FIELDS), :] = weight[pl.ds(corner, GROUPS, stride=8), :]


def pack(*operands):
    return pl.pallas_call(
        pack_kernel,
        out_shape=shape(GROUPS * FIELDS, CAP),
        in_specs=[pl.BlockSpec(memory_space=pl.ANY)] * 5,
        out_specs=VM,
        scratch_shapes=[pltpu.VMEM(a.shape, a.dtype) for a in operands] + [pltpu.SemaphoreType.DMA((5,))],
        compiler_params=pltpu.CompilerParams(vmem_limit_bytes=67_000_000),
        name="pack",
    )(*operands)


def unpack_kernel(velocity, returned, out):
    for axis in range(3):
        out[axis] = FLIP * velocity[axis] + returned[pl.ds(axis, GROUPS, stride=3), :]


def unpack(velocity, returned):
    return pl.pallas_call(
        unpack_kernel,
        out_shape=shape(3, GROUPS, CAP),
        in_specs=[VM] * 2,
        out_specs=VM,
        compiler_params=SMALL,
        name="unpack",
    )(velocity, returned)


def spread_kernel(msg, density, water, out, plane_s, depth_s, value_s, left_a, hot_a, left_b, hot_b, acc):
    cells_of(msg, plane_s, depth_s)
    depth_s[...] = depth_s[...].astype(F32).T.astype(jnp.int32)
    mass = msg[pl.ds(ROW_M, GROUPS, stride=FIELDS), :]
    value_s[0] = mass
    for axis in range(3):
        value_s[1 + axis] = mass * msg[pl.ds(axis, GROUPS, stride=FIELDS), :]
    acc[...] = jnp.zeros_like(acc)
    level = lax.broadcasted_iota(jnp.int32, (CAP, DEPTH), 1)

    def build(chunk, left, hot):
        depths = pltpu.roll(depth_s[...], (GROUPS - chunk * CHUNK) % GROUPS, 1)
        for j in range(CHUNK):
            source = chunk * CHUNK + j
            columns = slice(j * CAP, (j + 1) * CAP)
            weights = tile_weights(msg, source, plane_s[pl.ds(source, 1), :])
            for f in range(4):
                value = weights * value_s[f, pl.ds(source, 1), :]
                left[f * 64 : (f + 1) * 64, columns] = value
                left[256 + f * 64 : 256 + (f + 1) * 64, columns] = remainder(value)
            hot[columns, :] = jnp.where(level == depths[:, j : j + 1], 1.0, 0.0)

    def multiply(left, hot):
        acc[...] += one_pass(left[...], hot[...])

    turns = GROUPS // CHUNK
    build(0, left_a, hot_a)

    def body(turn, carry):
        build(2 * turn + 1, left_b, hot_b)
        multiply(left_a, hot_a)
        build((2 * turn + 2) & (turns - 1), left_a, hot_a)
        multiply(left_b, hot_b)
        return carry

    lax.fori_loop(0, turns // 2, body, 0)
    grid = []
    for f in range(4):
        both = acc[f * 64 : (f + 1) * 64, :] + acc[256 + f * 64 : 256 + (f + 1) * 64, :]
        grid.append(both[:CELLS] + pltpu.roll(both[CELLS:], 1, 1))
    total = grid[0] + density[...]
    out[0] = total
    for axis in range(3):
        out[1 + axis] = (grid[1 + axis] + density[...] * water[axis]) / total


def spread(msg, density, water):
    left = pltpu.VMEM((512, CHUNK * CAP), F32)
    hot = pltpu.VMEM((CHUNK * CAP, DEPTH), F32)
    index = pltpu.VMEM((GROUPS, CAP), jnp.int32)
    return pl.pallas_call(
        spread_kernel,
        out_shape=shape(4, CELLS, DEPTH),
        in_specs=[VM] * 3,
        out_specs=VM,
        scratch_shapes=[index, index, pltpu.VMEM((4, GROUPS, CAP), F32)]
        + [left, hot, left, hot]
        + [pltpu.VMEM((512, DEPTH), F32)],
        compiler_params=PARAMS,
        name="spread",
    )(msg, density, water)


def next_x(row):
    return pltpu.roll(row, XE - 1, 0)


def prev_x(row):
    return pltpu.roll(row, 1, 0)


def next_z(row):
    return pltpu.roll(row, DEPTH - 1, 1)


def prev_z(row):
    return pltpu.roll(row, 1, 1)


def each_row(first, last, body):
    def step(pair, carry):
        body(first + 2 * pair)
        body(first + 2 * pair + 1)
        return carry

    lax.fori_loop(0, (last - first) // 2, step, 0)
    if (last - first) % 2:
        body(last - 1)


def operate_row(field, y, offset, beta_x, beta_y, beta_z):
    here = field[y - offset]
    flux_x = beta_x[y] * (here - next_x(here))
    flux_z = beta_z[y] * (here - next_z(here))
    flux_y = beta_y[y] * (here - field[y - offset + 1])
    from_y = beta_y[y - 1] * (field[y - offset - 1] - here)
    return (
        DAMPING * here
        + (flux_x - prev_x(flux_x))
        + (flux_y - from_y)
        + (flux_z - prev_z(flux_z))
    )


def place(ext, corner, own, low_y, high_y, low_x, high_x, fix):
    for y in range(8):
        ext[HALO + y, 4:8, :] = own(slice(4 * y, 4 * y + 4))
    for y in range(HALO):
        rows = slice(4 * y, 4 * y + 4)
        ext[y, 4:8, :] = fix(low_y(rows), 1, 0)
        ext[HALO + 8 + y, 4:8, :] = fix(high_y(rows), 1, 2)
    for side, columns, source in ((0, slice(0, 4), low_x), (2, slice(8, 12), high_x)):
        for y in range(8):
            ext[HALO + y, columns, :] = fix(source(slice(4 * y, 4 * y + 4)), side, 1)
        for y in range(corner):
            first = CELLS + 4 * y
            ext[HALO - corner + y, columns, :] = fix(source(slice(first, first + 4)), side, 0)
            first = first + 4 * corner
            ext[HALO + 8 + y, columns, :] = fix(source(slice(first, first + 4)), side, 2)


def precondition(residual, inverse, beta_x, beta_y, beta_z, update, first, second, finish):
    theta = (UPPER + LOWER) / 2.0
    delta = (UPPER - LOWER) / 2.0
    sigma = theta / delta

    def start(y):
        value = inverse[y] * residual[y] * (1.0 / theta)
        update[y] = value
        first[y] = value

    each_row(1, YE - 1, start)
    previous = 1.0 / sigma
    current = 1.0 / (2.0 * sigma - previous)

    def middle(y):
        misfit = residual[y] - operate_row(first, y, 0, beta_x, beta_y, beta_z)
        value = current * previous * update[y] + (2.0 * current / delta) * inverse[y] * misfit
        update[y] = value
        second[y] = first[y] + value

    each_row(2, YE - 2, middle)
    latest = 1.0 / (2.0 * sigma - current)

    def last(y):
        misfit = residual[y] - operate_row(second, y, 0, beta_x, beta_y, beta_z)
        value = latest * current * update[y] + (2.0 * latest / delta) * inverse[y] * misfit
        finish(y, second[y] + value)

    each_row(3, YE - 3, last)


def each_pair(body):
    def step(pair, carry):
        y = HALO + 2 * pair
        rows = pl.ds(pl.multiple_of(8 * pair, 8), 8)
        lower_half = lax.broadcasted_iota(jnp.int32, (8, DEPTH), 0) < 4
        for ref, first, second in zip(*body(y)):
            ref[rows, :] = jnp.where(lower_half, pltpu.roll(first[:8], 4, 0), second[:8])
        return carry

    lax.fori_loop(0, 4, step, 0)


def start_kernel(
    edge, own, low_y, high_y, low_x, high_x,
    beta_x, beta_y, beta_z, inverse, basis, basis_own, image, source_own,
    ext, residual, update, first, second,
):
    infinite = jnp.full((4, DEPTH), jnp.inf, F32)
    for f in range(4):
        empty = jnp.inf if f == 0 else 0.0
        ext[f, :, 12:16, :] = jnp.full((YE, 4, DEPTH), empty, F32)
        for y in range(HALO - CORNER):
            for row in (y, YE - 1 - y):
                ext[f, row] = jnp.full((XE, DEPTH), empty, F32)

        def fix(value, column, row, f=f):
            if f:
                return value
            outside = 0
            if column != 1:
                outside = outside + edge[0 if column == 0 else 1]
            if row != 1:
                outside = outside + edge[2 if row == 0 else 3]
            return jnp.where(outside > 0, infinite, value)

        place(
            ext.at[f],
            CORNER,
            *[(lambda rows, ref=ref, f=f: ref[f, rows, :]) for ref in (own, low_y, high_y, low_x, high_x)],
            fix,
        )
    end = lax.broadcasted_iota(jnp.int32, (XE, DEPTH), 1) == DEPTH - 1

    def faces(y):
        total = ext[0, y]
        beta_x[y] = 2.0 / (total + next_x(total))
        beta_y[y] = 2.0 / (total + ext[0, y + 1])
        beta_z[y] = jnp.where(end, 0.0, 2.0 / (total + next_z(total)))

    each_row(0, YE - 1, faces)

    def source(y):
        across, along = beta_x[y], beta_z[y]
        diagonal = (
            DAMPING + across + prev_x(across) + beta_y[y] + beta_y[y - 1] + along + prev_z(along)
        )
        inverse[y] = 1.0 / diagonal
        vx, vy, vz = ext[1, y], ext[2, y], ext[3, y]
        flow_x = across * (vx + next_x(vx))
        flow_z = along * (vz + next_z(vz))
        flow_y = beta_y[y] * (vy + ext[2, y + 1]) - beta_y[y - 1] * (ext[2, y - 1] + vy)
        residual[y] = -0.5 * (
            (flow_x - prev_x(flow_x)) + flow_y + (flow_z - prev_z(flow_z))
        )

    each_row(1, YE - 1, source)

    def finish(y, value):
        basis[y - 3] = value

    precondition(residual, inverse, beta_x, beta_y, beta_z, update, first, second, finish)

    def apply(y):
        return operate_row(basis, y, 3, beta_x, beta_y, beta_z), basis[y - 3], residual[y]

    each_pair(lambda y: ((image, basis_own, source_own), apply(y), apply(y + 1)))


EXT = (YE, XE, DEPTH)
BASIS = (10, XE, DEPTH)
BLOCK = (CELLS, DEPTH)


def start_solve(edge, own, low_y, high_y, low_x, high_x):
    return pl.pallas_call(
        start_kernel,
        out_shape=[shape(*EXT)] * 4 + [shape(*BASIS)] + [shape(*BLOCK)] * 3,
        in_specs=[SM] + [VM] * 5,
        out_specs=[VM] * 8,
        scratch_shapes=[pltpu.VMEM((4,) + EXT, F32)] + [pltpu.VMEM(EXT, F32)] * 4,
        compiler_params=PARAMS,
        name="start_solve",
    )(edge, own, low_y, high_y, low_x, high_x)


def next_basis(own, low_y, high_y, low_x, high_x, betas, inverse, before, basis, basis_own, image, scratch):
    ext, update, first, second = scratch
    ext[:, 12:16, :] = jnp.zeros((YE, 4, DEPTH), F32)
    place(
        ext,
        HALO,
        *[(lambda rows, ref=ref: ref[rows, :]) for ref in (own, low_y, high_y, low_x, high_x)],
        lambda value, column, row: value,
    )

    def finish(y, value):
        basis[y - 3] = before[y - 3] - value

    precondition(ext, inverse, *betas, update, first, second, finish)

    def apply(y):
        return operate_row(basis, y, 3, *betas), basis[y - 3]

    each_pair(lambda y: ((image, basis_own), apply(y), apply(y + 1)))


def middle_kernel(
    own, low_y, high_y, low_x, high_x, beta_x, beta_y, beta_z, inverse, before,
    basis, basis_own, image, *scratch,
):
    next_basis(
        own, low_y, high_y, low_x, high_x, (beta_x, beta_y, beta_z), inverse, before,
        basis, basis_own, image, scratch,
    )


def last_kernel(
    own, low_y, high_y, low_x, high_x, beta_x, beta_y, beta_z, inverse, before,
    own_0, own_1, image_0, source_own, basis, sums, own_2, image_2, *scratch,
):
    next_basis(
        own, low_y, high_y, low_x, high_x, (beta_x, beta_y, beta_z), inverse, before,
        basis, own_2, image_2, scratch,
    )
    vectors = (own_0[...], own_1[...], own_2[...])
    images = (image_0[...], own[...], image_2[...])
    source = source_own[...]
    pairs = [(vectors[i], images[j]) for i in range(3) for j in range(i, 3)]
    pairs += [(vector, source) for vector in vectors]
    lane = lax.broadcasted_iota(jnp.int32, (1, CAP), 1)
    row = jnp.zeros((1, CAP), F32)
    for place_in, (a, b) in enumerate(pairs):
        folded = jnp.sum((a * b).reshape(4, 8, DEPTH), axis=0)
        folded = (folded[:, :128] + folded[:, 128:256]) + (folded[:, 256:384] + folded[:, 384:])
        row = jnp.where(lane == place_in, jnp.sum(folded, keepdims=True), row)
    sums[...] = jnp.broadcast_to(row, (GROUPS, CAP))


def middle_solve(own, low_y, high_y, low_x, high_x, betas, inverse, before):
    return pl.pallas_call(
        middle_kernel,
        out_shape=[shape(*BASIS), shape(*BLOCK), shape(*BLOCK)],
        in_specs=[VM] * 10,
        out_specs=[VM] * 3,
        scratch_shapes=[pltpu.VMEM(EXT, F32)] * 4,
        compiler_params=PARAMS,
        name="middle_solve",
    )(own, low_y, high_y, low_x, high_x, *betas, inverse, before)


def last_solve(own, low_y, high_y, low_x, high_x, betas, inverse, before, *inner):
    return pl.pallas_call(
        last_kernel,
        out_shape=[shape(*BASIS), shape(GROUPS, CAP)],
        in_specs=[VM] * 14,
        out_specs=[VM] * 2,
        scratch_shapes=[pltpu.VMEM(BLOCK, F32)] * 2 + [pltpu.VMEM(EXT, F32)] * 4,
        compiler_params=PARAMS,
        name="last_solve",
    )(own, low_y, high_y, low_x, high_x, *betas, inverse, before, *inner)


def coefficients(sums):
    total = jnp.sum(sums[...], axis=0, keepdims=True)
    g00, g01, g02, g11, g12, g22, b0, b1, b2 = [total[:, k : k + 1] for k in range(9)]
    l1 = g01 / g00
    l2 = g02 / g00
    d1 = g11 - l1 * g01
    keep_1 = d1 > 1e-7 * g11
    d1 = jnp.where(keep_1, d1, 1.0)
    m = jnp.where(keep_1, (g12 - l2 * g01) / d1, 0.0)
    d2 = g22 - l2 * g02 - m * m * d1
    keep_2 = d2 > 1e-7 * g22
    d2 = jnp.where(keep_2, d2, 1.0)
    y1 = b1 - l1 * b0
    y2 = b2 - l2 * b0 - m * y1
    c2 = jnp.where(keep_2, y2 / d2, 0.0)
    c1 = jnp.where(keep_1, y1 / d1, 0.0) - m * c2
    c0 = b0 / g00 - l1 * c1 - l2 * c2
    return c0, c1, c2


def gather_kernel(
    sums, basis_0, basis_1, basis_2, beta_x, beta_y, beta_z, own, msg,
    out, pressure_out, plane_s, depth_s, pressure, carried, table_s, hot_a, hot_b,
):
    c0, c1, c2 = [jnp.broadcast_to(c, (XE, DEPTH)) for c in coefficients(sums)]

    def combine(y):
        pressure[y] = c0 * basis_0[y] + c1 * basis_1[y] + c2 * basis_2[y]

    each_row(0, 10, combine)

    def slopes(y):
        here = pressure[y - 3]
        flux_x = beta_x[y] * (here - next_x(here))
        flux_z = beta_z[y] * (here - next_z(here))
        flux_y = beta_y[y] * (here - pressure[y - 2])
        from_y = beta_y[y - 1] * (pressure[y - 4] - here)
        return (
            (flux_x + prev_x(flux_x)) * 0.5,
            (flux_y + from_y) * 0.5,
            (flux_z + prev_z(flux_z)) * 0.5,
            here,
        )

    targets = (carried.at[0], carried.at[1], carried.at[2], pressure_out)
    each_pair(lambda y: (targets, slopes(y), slopes(y + 1)))
    for axis in range(3):
        velocity = own[1 + axis]
        value = (velocity + carried[axis]) - FLIP * velocity
        for lift, level in ((0, value), (1, next_z(value))):
            first = axis * 64 + lift * CELLS
            table_s[first : first + CELLS, :] = level
            table_s[192 + first : 192 + first + CELLS, :] = remainder(level)
    cells_of(msg, plane_s, depth_s)
    level = lax.broadcasted_iota(jnp.int32, (DEPTH, CAP), 0)

    def build(chunk, hot):
        for j in range(CHUNK):
            depth_row = depth_s[pl.ds(chunk * CHUNK + j, 1), :]
            hot[:, j * CAP : (j + 1) * CAP] = jnp.where(level == depth_row, 1.0, 0.0)

    def pick(chunk, hot):
        both = one_pass(table_s[...], hot[...])
        table = both[:192] + both[192:]
        for j in range(CHUNK):
            source = chunk * CHUNK + j
            weights = tile_weights(msg, source, plane_s[pl.ds(source, 1), :])
            for axis in range(3):
                picked = table[axis * 64 : (axis + 1) * 64, j * CAP : (j + 1) * CAP] * weights
                out[pl.ds(3 * source + axis, 1), :] = jnp.sum(picked, axis=0, keepdims=True)

    turns = GROUPS // CHUNK
    build(0, hot_a)

    def body(turn, carry):
        build(2 * turn + 1, hot_b)
        pick(2 * turn, hot_a)
        build((2 * turn + 2) & (turns - 1), hot_a)
        pick(2 * turn + 1, hot_b)
        return carry

    lax.fori_loop(0, turns // 2, body, 0)


def gather(sums, bases, betas, own, msg):
    index = pltpu.VMEM((GROUPS, CAP), jnp.int32)
    hot = pltpu.VMEM((DEPTH, CHUNK * CAP), F32)
    return pl.pallas_call(
        gather_kernel,
        out_shape=[shape(3 * GROUPS, CAP), shape(*BLOCK)],
        in_specs=[VM] * 9,
        out_specs=[VM] * 2,
        scratch_shapes=[index, index, pltpu.VMEM(BASIS, F32), pltpu.VMEM((3,) + BLOCK, F32), pltpu.VMEM((384, DEPTH), F32), hot, hot],
        compiler_params=PARAMS,
        name="gather",
    )(sums, *bases, *betas, own, msg)


def exchange(block, n_x, n_y, corner):
    up_x = [(i, (i + 1) % n_x) for i in range(n_x)]
    up_y = [(i, (i + 1) % n_y) for i in range(n_y)]
    down_x, down_y = [[(b, a) for a, b in up] for up in (up_x, up_y)]
    half = 4 * HALO
    low_y = lax.ppermute(block[..., CELLS - half :, :], "yz", up_y)
    high_y = lax.ppermute(block[..., :half, :], "yz", down_y)
    near = 4 * corner
    near_low, near_high = low_y, high_y
    if corner < HALO:
        near_low, near_high = low_y[..., half - near :, :], high_y[..., :near, :]
    column = jnp.concatenate([block, near_low, near_high], axis=-2)
    return low_y, high_y, lax.ppermute(column, "gx", up_x), lax.ppermute(column, "gx", down_x)


def by_block(field):
    turned = jnp.swapaxes(field, -3, -2)
    return turned.reshape(turned.shape[:-3] + (CELLS, DEPTH))


def local(part_mass, part_vel, corner_weight, corner_base, slot_counts, water_vel, solid_flag):
    n_x, n_y = lax.axis_size("gx"), lax.axis_size("yz")
    at_x, at_y = lax.axis_index("gx"), lax.axis_index("yz")
    edge = jnp.stack([at_x == 0, at_x == n_x - 1, at_y == 0, at_y == n_y - 1]).astype(jnp.int32)
    velocity = jnp.swapaxes(part_vel[0], 0, 1)
    message = pack(
        part_mass[0], velocity, corner_weight.reshape(8 * GROUPS, CAP), corner_base[0], slot_counts
    )
    msg = lax.all_to_all(message.reshape(GROUPS, 1, FIELDS * CAP), ALL, 0, 0, tiled=True)
    msg = msg.reshape(GROUPS * FIELDS, CAP)
    density = by_block(jnp.where(solid_flag == 1, SOLID_WATER, 1.0).astype(F32))
    own = spread(msg, density, by_block(water_vel))
    *rest, basis_0, own_0, image_0, source = start_solve(edge, own, *exchange(own, n_x, n_y, CORNER))
    betas, inverse = rest[:3], rest[3]
    basis_1, own_1, image_1 = middle_solve(image_0, *exchange(image_0, n_x, n_y, HALO), betas, inverse, basis_0)
    basis_2, sums = last_solve(
        image_1, *exchange(image_1, n_x, n_y, HALO), betas, inverse, basis_1, own_0, own_1, image_0, source
    )
    sums = lax.all_to_all(sums, ALL, 0, 0, tiled=True)
    sampled, pressure = gather(sums, (basis_0, basis_1, basis_2), betas, own, msg)
    returned = lax.all_to_all(sampled.reshape(GROUPS, 1, 3 * CAP), ALL, 0, 0, tiled=True)
    final = unpack(velocity, returned.reshape(3 * GROUPS, CAP))
    pressure = jnp.swapaxes(pressure.reshape(8, 4, DEPTH), 0, 1)
    return jnp.swapaxes(final, 0, 1)[None], pressure


def solution(mesh):
    parts = P(ALL, None, None)
    in_specs = (parts, P(ALL, None, None, None), P(ALL, None, None, None), parts, P(ALL, None), P(None, "gx", "yz", None), P("gx", "yz", None))
    out_specs = (P(ALL, None, None, None), P("gx", "yz", None))
    return jax.shard_map(local, mesh=mesh, in_specs=in_specs, out_specs=out_specs, check_vma=False)
```

```python
import jax
import jax.numpy as jnp
from jax import lax
from jax.experimental import pallas as pl
from jax.experimental.pallas import tpu as pltpu
from jax.sharding import PartitionSpec as P

ALL = ("gx", "yz")
DAMPING = 0.05
SOLID_WATER = 0.1
FLIP = 0.9
LOWER = 0.1
UPPER = 2.0
DEGREE = 3
GROUPS = 128
CAP = 128
FIELDS = 13
ROW_W = 3
ROW_M = 11
ROW_B = 12
CELLS = 32
DEPTH = 512
CHUNK = 8
HALO = 4
UNROLL = 4
WIDE = 6
YW = 8 + 2 * WIDE
CORNER = 3
YE = 8 + 2 * HALO
XE = 16
PARAMS = pltpu.CompilerParams(vmem_limit_bytes=20 * 1024 * 1024)
SMALL = pltpu.CompilerParams(vmem_limit_bytes=8 * 1024 * 1024)
VM = pl.BlockSpec(memory_space=pltpu.VMEM)
SM = pl.BlockSpec(memory_space=pltpu.SMEM)
F32 = jnp.float32
BF16 = jnp.bfloat16


def shape(*dims):
    return jax.ShapeDtypeStruct(dims, F32)


def remainder(value):
    return value - value.astype(BF16).astype(F32)


def one_pass(left, right):
    return lax.dot_general(
        left, right, (((1,), (0,)), ((), ())), precision=lax.Precision.DEFAULT, preferred_element_type=F32
    )


def cells_of(msg, plane_s, depth_s):
    base = msg[pl.ds(ROW_B, GROUPS, stride=FIELDS), :].astype(jnp.int32)
    plane = base >> 9
    plane_s[...] = (plane & 7) * 4 + (plane >> 3)
    depth_s[...] = base & 511


def tile_weights(msg, source, plane_row):
    away = lax.broadcasted_iota(jnp.int32, (CELLS, CAP), 0) - plane_row
    here, next_y, next_x, next_xy = away == 0, away == 4, away == 1, away == 5
    zero = jnp.zeros((CELLS, CAP), F32)

    def weight(corner):
        row = msg[pl.ds(FIELDS * source + ROW_W + corner, 1), :]
        return jnp.broadcast_to(row, (CELLS, CAP))

    lifts = []
    for lift in (0, 1):
        value = jnp.where(next_xy, weight(6 + lift), zero)
        value = jnp.where(next_x, weight(4 + lift), value)
        value = jnp.where(next_y, weight(2 + lift), value)
        lifts.append(jnp.where(here, weight(lift), value))
    return jnp.concatenate(lifts, axis=0)


def pack_kernel(mass_h, velocity_h, weight_h, base_h, count_h, out, mass, velocity, weight, base, count, sems):
    pairs = ((count_h, count), (mass_h, mass), (base_h, base), (velocity_h, velocity), (weight_h, weight))
    copies = [pltpu.make_async_copy(a, b, sems.at[k]) for k, (a, b) in enumerate(pairs)]
    for copy in copies:
        copy.start()
    copies[0].wait()
    limit = jnp.broadcast_to(count[...], (GROUPS, CAP)).astype(F32).T
    slot = lax.broadcasted_iota(jnp.int32, (GROUPS, CAP), 1).astype(F32)
    live = jnp.where(slot < limit, 1.0, 0.0)
    copies[1].wait()
    out[pl.ds(ROW_M, GROUPS, stride=FIELDS), :] = mass[...] * live
    copies[2].wait()
    out[pl.ds(ROW_B, GROUPS, stride=FIELDS), :] = base[...].astype(F32)
    copies[3].wait()
    for axis in range(3):
        out[pl.ds(axis, GROUPS, stride=FIELDS), :] = velocity[axis]
    copies[4].wait()
    for corner in range(8):
        out[pl.ds(ROW_W + corner, GROUPS, stride=FIELDS), :] = weight[pl.ds(corner, GROUPS, stride=8), :]


def pack(*operands):
    return pl.pallas_call(
        pack_kernel,
        out_shape=shape(GROUPS * FIELDS, CAP),
        in_specs=[pl.BlockSpec(memory_space=pl.ANY)] * 5,
        out_specs=VM,
        scratch_shapes=[pltpu.VMEM(a.shape, a.dtype) for a in operands] + [pltpu.SemaphoreType.DMA((5,))],
        compiler_params=pltpu.CompilerParams(vmem_limit_bytes=67_000_000),
        name="pack",
    )(*operands)


def unpack_kernel(velocity, returned, out):
    for axis in range(3):
        out[axis] = FLIP * velocity[axis] + returned[pl.ds(axis, GROUPS, stride=3), :]


def unpack(velocity, returned):
    return pl.pallas_call(
        unpack_kernel,
        out_shape=shape(3, GROUPS, CAP),
        in_specs=[VM] * 2,
        out_specs=VM,
        compiler_params=SMALL,
        name="unpack",
    )(velocity, returned)


def spread_kernel(msg, density, water, out, plane_s, depth_s, value_s, left_a, hot_a, left_b, hot_b, acc):
    cells_of(msg, plane_s, depth_s)
    depth_s[...] = depth_s[...].astype(F32).T.astype(jnp.int32)
    mass = msg[pl.ds(ROW_M, GROUPS, stride=FIELDS), :]
    value_s[0] = mass
    for axis in range(3):
        value_s[1 + axis] = mass * msg[pl.ds(axis, GROUPS, stride=FIELDS), :]
    acc[...] = jnp.zeros_like(acc)
    level = lax.broadcasted_iota(jnp.int32, (CAP, DEPTH), 1)

    def build(chunk, left, hot):
        depths = pltpu.roll(depth_s[...], (GROUPS - chunk * CHUNK) % GROUPS, 1)
        for j in range(CHUNK):
            source = chunk * CHUNK + j
            columns = slice(j * CAP, (j + 1) * CAP)
            weights = tile_weights(msg, source, plane_s[pl.ds(source, 1), :])
            for f in range(4):
                value = weights * value_s[f, pl.ds(source, 1), :]
                left[f * 64 : (f + 1) * 64, columns] = value
                left[256 + f * 64 : 256 + (f + 1) * 64, columns] = remainder(value)
            hot[columns, :] = jnp.where(level == depths[:, j : j + 1], 1.0, 0.0)

    def multiply(left, hot):
        acc[...] += one_pass(left[...], hot[...])

    turns = GROUPS // CHUNK
    build(0, left_a, hot_a)

    def body(turn, carry):
        build(2 * turn + 1, left_b, hot_b)
        multiply(left_a, hot_a)
        build((2 * turn + 2) & (turns - 1), left_a, hot_a)
        multiply(left_b, hot_b)
        return carry

    lax.fori_loop(0, turns // 2, body, 0)
    grid = []
    for f in range(4):
        both = acc[f * 64 : (f + 1) * 64, :] + acc[256 + f * 64 : 256 + (f + 1) * 64, :]
        grid.append(both[:CELLS] + pltpu.roll(both[CELLS:], 1, 1))
    total = grid[0] + density[...]
    out[0] = total
    for axis in range(3):
        out[1 + axis] = (grid[1 + axis] + density[...] * water[axis]) / total


def spread(msg, density, water):
    left = pltpu.VMEM((512, CHUNK * CAP), F32)
    hot = pltpu.VMEM((CHUNK * CAP, DEPTH), F32)
    index = pltpu.VMEM((GROUPS, CAP), jnp.int32)
    return pl.pallas_call(
        spread_kernel,
        out_shape=shape(4, CELLS, DEPTH),
        in_specs=[VM] * 3,
        out_specs=VM,
        scratch_shapes=[index, index, pltpu.VMEM((4, GROUPS, CAP), F32)]
        + [left, hot, left, hot]
        + [pltpu.VMEM((512, DEPTH), F32)],
        compiler_params=PARAMS,
        name="spread",
    )(msg, density, water)


def next_x(row):
    return pltpu.roll(row, XE - 1, 0)


def prev_x(row):
    return pltpu.roll(row, 1, 0)


def next_z(row):
    return pltpu.roll(row, DEPTH - 1, 1)


def prev_z(row):
    return pltpu.roll(row, 1, 1)


def each_row(first, last, body):
    turns, rest = divmod(last - first, UNROLL)

    def step(turn, carry):
        for k in range(UNROLL):
            body(first + UNROLL * turn + k)
        return carry

    lax.fori_loop(0, turns, step, 0)
    for k in range(rest):
        body(last - rest + k)


def operate_row(field, y, offset, beta_x, beta_y, beta_z):
    here = field[y - offset]
    flux_x = beta_x[y] * (here - next_x(here))
    flux_z = beta_z[y] * (here - next_z(here))
    flux_y = beta_y[y] * (here - field[y - offset + 1])
    from_y = beta_y[y - 1] * (field[y - offset - 1] - here)
    return (
        DAMPING * here
        + (flux_x - prev_x(flux_x))
        + (flux_y - from_y)
        + (flux_z - prev_z(flux_z))
    )


def place(ext, corner, own, low_y, high_y, low_x, high_x, fix):
    for y in range(8):
        ext[HALO + y, 4:8, :] = own(slice(4 * y, 4 * y + 4))
    for y in range(HALO):
        rows = slice(4 * y, 4 * y + 4)
        ext[y, 4:8, :] = fix(low_y(rows), 1, 0)
        ext[HALO + 8 + y, 4:8, :] = fix(high_y(rows), 1, 2)
    for side, columns, source in ((0, slice(0, 4), low_x), (2, slice(8, 12), high_x)):
        for y in range(8):
            ext[HALO + y, columns, :] = fix(source(slice(4 * y, 4 * y + 4)), side, 1)
        for y in range(corner):
            first = CELLS + 4 * y
            ext[HALO - corner + y, columns, :] = fix(source(slice(first, first + 4)), side, 0)
            first = first + 4 * corner
            ext[HALO + 8 + y, columns, :] = fix(source(slice(first, first + 4)), side, 2)


def precondition(scaled, inverse, betas, update, first, second, finish, low, high):
    theta = (UPPER + LOWER) / 2.0
    delta = (UPPER - LOWER) / 2.0
    sigma = theta / delta

    def start(y):
        value = scaled[y] * (1.0 / theta)
        update[y] = value
        first[y] = value

    each_row(low, high, start)
    previous = 1.0 / sigma
    current = 1.0 / (2.0 * sigma - previous)

    def middle(y):
        misfit = scaled[y] - inverse[y] * operate_row(first, y, 0, *betas)
        value = current * previous * update[y] + (2.0 * current / delta) * misfit
        update[y] = value
        second[y] = first[y] + value

    each_row(low + 1, high - 1, middle)
    latest = 1.0 / (2.0 * sigma - current)

    def last(y):
        misfit = scaled[y] - inverse[y] * operate_row(second, y, 0, *betas)
        value = latest * current * update[y] + (2.0 * latest / delta) * misfit
        finish(y, second[y] + value)

    each_row(low + 2, high - 2, last)


def each_pair(base, body):
    def step(pair, carry):
        y = base + 2 * pair
        rows = pl.ds(pl.multiple_of(8 * pair, 8), 8)
        lower_half = lax.broadcasted_iota(jnp.int32, (8, DEPTH), 0) < 4
        for ref, first, second in zip(*body(y)):
            ref[rows, :] = jnp.where(lower_half, pltpu.roll(first[:8], 4, 0), second[:8])
        return carry

    lax.fori_loop(0, 4, step, 0)


def outside_fix(edge, infinite, value, column, row):
    outside = 0
    if column != 1:
        outside = outside + edge[0 if column == 0 else 1]
    if row != 1:
        outside = outside + edge[2 if row == 0 else 3]
    return jnp.where(outside > 0, infinite, value)


def face_row(total, y, end, cut, beta_x, beta_y, beta_z):
    here = total[y]
    across = 2.0 / (here + next_x(here))
    beta_x[y] = across if cut is None else jnp.where(cut, 0.0, across)
    beta_y[y] = 2.0 / (here + total[y + 1])
    beta_z[y] = jnp.where(end, 0.0, 2.0 / (here + next_z(here)))


def inverse_row(y, beta_x, beta_y, beta_z):
    across, along = beta_x[y], beta_z[y]
    return 1.0 / (
        DAMPING + across + prev_x(across) + beta_y[y] + beta_y[y - 1] + along + prev_z(along)
    )


def start_kernel(
    edge, own, low_y, high_y, low_x, high_x,
    basis, basis_own, image, scaled_own, source_own, total, up, down,
    ext, residual, scaled, beta_x, beta_y, beta_z, inverse, update, first, second,
):
    infinite = jnp.full((4, DEPTH), jnp.inf, F32)
    for f in range(4):
        target = ext.at[f - 1] if f else total
        empty = 0.0 if f else jnp.inf
        target[:, 12:16, :] = jnp.full((YE, 4, DEPTH), empty, F32)
        for y in range(HALO - CORNER):
            for row in (y, YE - 1 - y):
                target[row] = jnp.full((XE, DEPTH), empty, F32)

        def fix(value, column, row, f=f):
            return outside_fix(edge, infinite, value, column, row) if f == 0 else value

        place(
            target,
            CORNER,
            *[(lambda rows, ref=ref, f=f: ref[f, rows, :]) for ref in (own, low_y, high_y, low_x, high_x)],
            fix,
        )
    end = lax.broadcasted_iota(jnp.int32, (XE, DEPTH), 1) == DEPTH - 1
    betas = (beta_x, beta_y, beta_z)
    each_row(0, YE - 1, lambda y: face_row(total, y, end, None, *betas))

    def source(y):
        weight = inverse_row(y, *betas)
        inverse[y] = weight
        vx, vy, vz = ext[0, y], ext[1, y], ext[2, y]
        flow_x = beta_x[y] * (vx + next_x(vx))
        flow_z = beta_z[y] * (vz + next_z(vz))
        flow_y = beta_y[y] * (vy + ext[1, y + 1]) - beta_y[y - 1] * (ext[1, y - 1] + vy)
        value = -0.5 * ((flow_x - prev_x(flow_x)) + flow_y + (flow_z - prev_z(flow_z)))
        residual[y] = value
        scaled[y] = weight * value

    each_row(1, YE - 1, source)

    def finish(y, value):
        basis[y - 3] = value

    precondition(scaled, inverse, betas, update, first, second, finish, 1, YE - 1)

    def apply(y):
        value = operate_row(basis, y, 3, *betas)
        return value, basis[y - 3], residual[y], inverse[y] * value

    each_pair(HALO, lambda y: ((image, basis_own, source_own, scaled_own), apply(y), apply(y + 1)))
    up[:24, :] = scaled_own[8:, :]
    up[24:, :] = own[0, 8:16, :]
    down[:24, :] = scaled_own[:24, :]
    down[24:, :] = own[0, 16:24, :]


EXT = (YE, XE, DEPTH)
BROAD = (YW, XE, DEPTH)
BASIS = (10, XE, DEPTH)
BLOCK = (CELLS, DEPTH)


def start_solve(edge, own, near):
    return pl.pallas_call(
        start_kernel,
        out_shape=[shape(*BASIS)] + [shape(*BLOCK)] * 4 + [shape(*EXT)] + [shape(*BLOCK)] * 2,
        in_specs=[SM] + [VM] * 5,
        out_specs=[VM] * 8,
        scratch_shapes=[pltpu.VMEM((3,) + EXT, F32)] + [pltpu.VMEM(EXT, F32)] * 9,
        compiler_params=PARAMS,
        name="start_solve",
    )(edge, own, *near)


def four(index):
    return slice(4 * index, 4 * index + 4)


def two(index):
    return slice(2 * index, 2 * index + 2)


def solve_kernel(
    edge, total_near, scaled_own, wide_ly, wide_hy, wide_lx, wide_hx, far_lx, far_hx,
    basis_0, own_0, image_0, source_own,
    basis_1, basis_2, out_x, out_y, out_z, sums,
    total, scaled, beta_x, beta_y, beta_z, inverse, update, first, second, vector, scaled_1, vector_2,
    own_1, image_1, own_2, image_2,
):
    infinite = jnp.full((4, DEPTH), jnp.inf, F32)
    for y in range(YE):
        total[y + 2] = total_near[y]
    for y in range(YW):
        if y < 2 or y >= YW - 2:
            total[y] = jnp.full((XE, DEPTH), jnp.inf, F32)
        scaled[y] = jnp.zeros((XE, DEPTH), F32)

    def put(y, columns, value, column):
        row = 0 if y < WIDE else 2
        total[y, columns, :] = outside_fix(edge, infinite, value, column, row)

    middle = slice(4, 8)
    for y in range(8):
        scaled[WIDE + y, middle, :] = scaled_own[four(y), :]
    for y in range(WIDE):
        scaled[y, middle, :] = wide_ly[four(y), :]
        scaled[WIDE + 8 + y, middle, :] = wide_hy[four(y), :]
    for y in range(2):
        put(y, middle, wide_ly[four(WIDE + y), :], 1)
        put(WIDE + 12 + y, middle, wide_hy[four(WIDE + y), :], 1)
    for side, columns, wide in ((0, slice(0, 4), wide_lx), (2, slice(8, 12), wide_hx)):
        for y in range(8):
            scaled[WIDE + y, columns, :] = wide[four(y), :]
        for y in range(5):
            scaled[1 + y, columns, :] = wide[four(8 + y), :]
            scaled[WIDE + 8 + y, columns, :] = wide[four(13 + y), :]
        for place_in, y in enumerate((1, 2, WIDE + 11, WIDE + 12)):
            put(y, columns, wide[four(18 + place_in), :], side)
    for flag, columns, far in ((4, slice(14, 16), far_lx), (5, slice(12, 14), far_hx)):
        for y in range(10):
            row = 0 if y == 0 else (2 if y == 9 else 1)
            outside = edge[flag]
            if row != 1:
                outside = outside + edge[2 if row == 0 else 3]
            value = far[two(10 + y), :]
            total[WIDE - 1 + y, columns, :] = jnp.where(outside > 0, infinite[:2], value)
            scaled[WIDE - 1 + y, columns, :] = far[two(y), :]

    end = lax.broadcasted_iota(jnp.int32, (XE, DEPTH), 1) == DEPTH - 1
    cut = lax.broadcasted_iota(jnp.int32, (XE, DEPTH), 0) == 13
    betas = (beta_x, beta_y, beta_z)
    each_row(0, YW - 1, lambda y: face_row(total, y, end, cut, *betas))

    def invert(y):
        inverse[y] = inverse_row(y, *betas)

    each_row(1, YW - 1, invert)

    def finish_1(y, value):
        vector[y] = value

    precondition(scaled, inverse, betas, update, first, second, finish_1, 0, YW)

    def rescale(y):
        value = operate_row(vector, y, 0, *betas)
        second[y] = value
        scaled_1[y] = inverse[y] * value

    each_row(3, YW - 3, rescale)
    each_pair(WIDE, lambda y: ((own_1, image_1), (vector[y], second[y]), (vector[y + 1], second[y + 1])))

    def finish_2(y, value):
        before = basis_0[y - 5]
        vector_2[y - 5] = value
        basis_1[y - 5] = before - vector[y]
        basis_2[y - 5] = (before - vector[y]) - (vector[y] - value)
        out_x[y - 5] = beta_x[y]
        out_y[y - 5] = beta_y[y]
        out_z[y - 5] = beta_z[y]

    precondition(scaled_1, inverse, betas, update, first, second, finish_2, 3, YW - 3)

    def apply(y):
        return vector_2[y - 5], operate_row(vector_2, y, 5, *betas)

    each_pair(WIDE, lambda y: ((own_2, image_2), apply(y), apply(y + 1)))
    v0, v1, v2 = own_0[...], own_1[...], own_2[...]
    a0, a1, a2 = image_0[...], image_1[...], image_2[...]
    vectors = (v0, v0 - v1, (v0 - v1) - (v1 - v2))
    images = (a0, a0 - a1, (a0 - a1) - (a1 - a2))
    source = source_own[...]
    pairs = [(vectors[i], images[j]) for i in range(3) for j in range(i, 3)]
    pairs += [(item, source) for item in vectors]
    lane = lax.broadcasted_iota(jnp.int32, (1, CAP), 1)
    row = jnp.zeros((1, CAP), F32)
    for place_in, (a, b) in enumerate(pairs):
        folded = jnp.sum((a * b).reshape(4, 8, DEPTH), axis=0)
        folded = (folded[:, :128] + folded[:, 128:256]) + (folded[:, 256:384] + folded[:, 384:])
        row = jnp.where(lane == place_in, jnp.sum(folded, keepdims=True), row)
    sums[...] = jnp.broadcast_to(row, (GROUPS, CAP))


def widen_kernel(block, low_y, high_y, total, column, far_up, far_down):
    column[:32, :] = block[...]
    column[32:52, :] = low_y[4:24, :]
    column[52:72, :] = high_y[:20, :]
    column[72:76, :] = low_y[28:32, :]
    column[76:80, :] = total[0, 4:8, :]
    column[80:84, :] = total[YE - 1, 4:8, :]
    column[84:88, :] = high_y[24:28, :]
    for first, target in ((2, far_up), (0, far_down)):
        target[two(0), :] = low_y[20 + first : 22 + first, :]
        for y in range(8):
            target[two(1 + y), :] = block[4 * y + first : 4 * y + first + 2, :]
        target[two(9), :] = high_y[first : first + 2, :]
        for y in range(10):
            target[two(10 + y), :] = total[HALO - 1 + y, 4 + first : 6 + first, :]


def widen(block, low_y, high_y, total):
    return pl.pallas_call(
        widen_kernel,
        out_shape=[shape(88, DEPTH), shape(40, DEPTH), shape(40, DEPTH)],
        in_specs=[VM] * 4,
        out_specs=[VM] * 3,
        compiler_params=SMALL,
        name="widen",
    )(block, low_y, high_y, total)


def solve(edge, total, scaled, wide, basis_0, *inner):
    return pl.pallas_call(
        solve_kernel,
        out_shape=[shape(*BASIS)] * 5 + [shape(GROUPS, CAP)],
        in_specs=[SM] + [VM] * 12,
        out_specs=[VM] * 6,
        scratch_shapes=[pltpu.VMEM(BROAD, F32)] * 11
        + [pltpu.VMEM(BASIS, F32)]
        + [pltpu.VMEM(BLOCK, F32)] * 4,
        compiler_params=PARAMS,
        name="solve",
    )(edge, total, scaled, *wide, basis_0, *inner)


def coefficients(sums):
    total = jnp.sum(sums[...], axis=0, keepdims=True)
    g00, g01, g02, g11, g12, g22, b0, b1, b2 = [total[:, k : k + 1] for k in range(9)]
    l1 = g01 / g00
    l2 = g02 / g00
    d1 = g11 - l1 * g01
    keep_1 = d1 > 1e-7 * g11
    d1 = jnp.where(keep_1, d1, 1.0)
    m = jnp.where(keep_1, (g12 - l2 * g01) / d1, 0.0)
    d2 = g22 - l2 * g02 - m * m * d1
    keep_2 = d2 > 1e-7 * g22
    d2 = jnp.where(keep_2, d2, 1.0)
    y1 = b1 - l1 * b0
    y2 = b2 - l2 * b0 - m * y1
    c2 = jnp.where(keep_2, y2 / d2, 0.0)
    c1 = jnp.where(keep_1, y1 / d1, 0.0) - m * c2
    c0 = b0 / g00 - l1 * c1 - l2 * c2
    return c0, c1, c2


def gather_kernel(
    sums, basis_0, basis_1, basis_2, beta_x, beta_y, beta_z, own, msg,
    out, pressure_out, plane_s, depth_s, pressure, carried, table_s, hot_a, hot_b,
):
    c0, c1, c2 = [jnp.broadcast_to(c, (XE, DEPTH)) for c in coefficients(sums)]

    def combine(y):
        pressure[y] = c0 * basis_0[y] + c1 * basis_1[y] + c2 * basis_2[y]

    each_row(0, 10, combine)

    def slopes(y):
        here = pressure[y]
        flux_x = beta_x[y] * (here - next_x(here))
        flux_z = beta_z[y] * (here - next_z(here))
        flux_y = beta_y[y] * (here - pressure[y + 1])
        from_y = beta_y[y - 1] * (pressure[y - 1] - here)
        return (
            (flux_x + prev_x(flux_x)) * 0.5,
            (flux_y + from_y) * 0.5,
            (flux_z + prev_z(flux_z)) * 0.5,
            here,
        )

    targets = (carried.at[0], carried.at[1], carried.at[2], pressure_out)
    each_pair(1, lambda y: (targets, slopes(y), slopes(y + 1)))
    for axis in range(3):
        velocity = own[1 + axis]
        value = (velocity + carried[axis]) - FLIP * velocity
        for lift, level in ((0, value), (1, next_z(value))):
            first = axis * 64 + lift * CELLS
            table_s[first : first + CELLS, :] = level
            table_s[192 + first : 192 + first + CELLS, :] = remainder(level)
    cells_of(msg, plane_s, depth_s)
    level = lax.broadcasted_iota(jnp.int32, (DEPTH, CAP), 0)

    def build(chunk, hot):
        for j in range(CHUNK):
            depth_row = depth_s[pl.ds(chunk * CHUNK + j, 1), :]
            hot[:, j * CAP : (j + 1) * CAP] = jnp.where(level == depth_row, 1.0, 0.0)

    def pick(chunk, hot):
        both = one_pass(table_s[...], hot[...])
        table = both[:192] + both[192:]
        for j in range(CHUNK):
            source = chunk * CHUNK + j
            weights = tile_weights(msg, source, plane_s[pl.ds(source, 1), :])
            for axis in range(3):
                picked = table[axis * 64 : (axis + 1) * 64, j * CAP : (j + 1) * CAP] * weights
                out[pl.ds(3 * source + axis, 1), :] = jnp.sum(picked, axis=0, keepdims=True)

    turns = GROUPS // CHUNK
    build(0, hot_a)

    def body(turn, carry):
        build(2 * turn + 1, hot_b)
        pick(2 * turn, hot_a)
        build((2 * turn + 2) & (turns - 1), hot_a)
        pick(2 * turn + 1, hot_b)
        return carry

    lax.fori_loop(0, turns // 2, body, 0)


def gather(sums, bases, betas, own, msg):
    index = pltpu.VMEM((GROUPS, CAP), jnp.int32)
    hot = pltpu.VMEM((DEPTH, CHUNK * CAP), F32)
    return pl.pallas_call(
        gather_kernel,
        out_shape=[shape(3 * GROUPS, CAP), shape(*BLOCK)],
        in_specs=[VM] * 9,
        out_specs=[VM] * 2,
        scratch_shapes=[index, index, pltpu.VMEM(BASIS, F32), pltpu.VMEM((3,) + BLOCK, F32), pltpu.VMEM((384, DEPTH), F32), hot, hot],
        compiler_params=PARAMS,
        name="gather",
    )(sums, *bases, *betas, own, msg)


def exchange(block, n_x, n_y, corner):
    up_x = [(i, (i + 1) % n_x) for i in range(n_x)]
    up_y = [(i, (i + 1) % n_y) for i in range(n_y)]
    down_x, down_y = [[(b, a) for a, b in up] for up in (up_x, up_y)]
    half = 4 * HALO
    low_y = lax.ppermute(block[..., CELLS - half :, :], "yz", up_y)
    high_y = lax.ppermute(block[..., :half, :], "yz", down_y)
    near = 4 * corner
    near_low, near_high = low_y, high_y
    if corner < HALO:
        near_low, near_high = low_y[..., half - near :, :], high_y[..., :near, :]
    column = jnp.concatenate([block, near_low, near_high], axis=-2)
    return low_y, high_y, lax.ppermute(column, "gx", up_x), lax.ppermute(column, "gx", down_x)


def exchange_wide(block, up, down, total, n_x, n_y):
    up_x, up_xx = [[(i, (i + k) % n_x) for i in range(n_x)] for k in (1, 2)]
    up_y = [(i, (i + 1) % n_y) for i in range(n_y)]
    down_x, down_xx, down_y = [[(b, a) for a, b in pairs] for pairs in (up_x, up_xx, up_y)]
    low_y = lax.ppermute(up, "yz", up_y)
    high_y = lax.ppermute(down, "yz", down_y)
    column, far_up, far_down = widen(block, low_y, high_y, total)
    far_lx = lax.ppermute(far_up, "gx", up_xx)
    far_hx = lax.ppermute(far_down, "gx", down_xx)
    low_x = lax.ppermute(column, "gx", up_x)
    high_x = lax.ppermute(column, "gx", down_x)
    return low_y, high_y, low_x, high_x, far_lx, far_hx


def by_block(field):
    turned = jnp.swapaxes(field, -3, -2)
    return turned.reshape(turned.shape[:-3] + (CELLS, DEPTH))


def local(part_mass, part_vel, corner_weight, corner_base, slot_counts, water_vel, solid_flag):
    n_x, n_y = lax.axis_size("gx"), lax.axis_size("yz")
    at_x, at_y = lax.axis_index("gx"), lax.axis_index("yz")
    edge = jnp.stack(
        [at_x == 0, at_x == n_x - 1, at_y == 0, at_y == n_y - 1, at_x <= 1, at_x >= n_x - 2]
    ).astype(jnp.int32)
    velocity = jnp.swapaxes(part_vel[0], 0, 1)
    message = pack(
        part_mass[0], velocity, corner_weight.reshape(8 * GROUPS, CAP), corner_base[0], slot_counts
    )
    msg = lax.all_to_all(message.reshape(GROUPS, 1, FIELDS * CAP), ALL, 0, 0, tiled=True)
    msg = msg.reshape(GROUPS * FIELDS, CAP)
    density = by_block(jnp.where(solid_flag == 1, SOLID_WATER, 1.0).astype(F32))
    own = spread(msg, density, by_block(water_vel))
    near = exchange(own, n_x, n_y, CORNER)
    basis_0, own_0, image_0, scaled, source, total, up, down = start_solve(edge, own, near)
    wide = exchange_wide(scaled, up, down, total, n_x, n_y)
    basis_1, basis_2, *betas, sums = solve(
        edge, total, scaled, wide, basis_0, own_0, image_0, source
    )
    sums = lax.all_to_all(sums, ALL, 0, 0, tiled=True)
    sampled, pressure = gather(sums, (basis_0, basis_1, basis_2), betas, own, msg)
    returned = lax.all_to_all(sampled.reshape(GROUPS, 1, 3 * CAP), ALL, 0, 0, tiled=True)
    final = unpack(velocity, returned.reshape(3 * GROUPS, CAP))
    pressure = jnp.swapaxes(pressure.reshape(8, 4, DEPTH), 0, 1)
    return jnp.swapaxes(final, 0, 1)[None], pressure


def solution(mesh):
    parts = P(ALL, None, None)
    in_specs = (parts, P(ALL, None, None, None), P(ALL, None, None, None), parts, P(ALL, None), P(None, "gx", "yz", None), P("gx", "yz", None))
    out_specs = (P(ALL, None, None, None), P("gx", "yz", None))
    return jax.shard_map(local, mesh=mesh, in_specs=in_specs, out_specs=out_specs, check_vma=False)
```

```python
import jax
import jax.numpy as jnp
from jax import lax
from jax.experimental import pallas as pl
from jax.experimental.pallas import tpu as pltpu
from jax.sharding import PartitionSpec as P

ALL = ("gx", "yz")
DAMPING = 0.05
SOLID_WATER = 0.1
FLIP = 0.9
LOWER = 0.1
UPPER = 2.0
DEGREE = 3
GROUPS = 128
CAP = 128
FIELDS = 13
ROW_W = 3
ROW_M = 11
ROW_B = 12
CELLS = 32
DEPTH = 512
CHUNK = 8
PICK = 16
HALO = 4
UNROLL = 4
WIDE = 6
YW = 8 + 2 * WIDE
CORNER = 3
YE = 8 + 2 * HALO
XE = 16
PARAMS = pltpu.CompilerParams(vmem_limit_bytes=20 * 1024 * 1024)
LARGE = pltpu.CompilerParams(vmem_limit_bytes=28 * 1024 * 1024)
SMALL = pltpu.CompilerParams(vmem_limit_bytes=8 * 1024 * 1024)
VM = pl.BlockSpec(memory_space=pltpu.VMEM)
SM = pl.BlockSpec(memory_space=pltpu.SMEM)
F32 = jnp.float32
BF16 = jnp.bfloat16


def shape(*dims):
    return jax.ShapeDtypeStruct(dims, F32)


def remainder(value):
    return value - value.astype(BF16).astype(F32)


def one_pass(left, right):
    return lax.dot_general(
        left, right, (((1,), (0,)), ((), ())), precision=lax.Precision.DEFAULT, preferred_element_type=F32
    )


def cells_of(msg, plane_s, depth_s):
    base = msg[pl.ds(ROW_B, GROUPS, stride=FIELDS), :].astype(jnp.int32)
    plane = base >> 9
    plane_s[...] = (plane & 7) * 4 + (plane >> 3)
    depth_s[...] = base & 511


def tile_weights(msg, source, plane_row):
    away = lax.broadcasted_iota(jnp.int32, (CELLS, CAP), 0) - plane_row
    here, next_y, next_x, next_xy = away == 0, away == 4, away == 1, away == 5
    zero = jnp.zeros((CELLS, CAP), F32)

    def weight(corner):
        row = msg[pl.ds(FIELDS * source + ROW_W + corner, 1), :]
        return jnp.broadcast_to(row, (CELLS, CAP))

    lifts = []
    for lift in (0, 1):
        value = jnp.where(next_xy, weight(6 + lift), zero)
        value = jnp.where(next_x, weight(4 + lift), value)
        value = jnp.where(next_y, weight(2 + lift), value)
        lifts.append(jnp.where(here, weight(lift), value))
    return jnp.concatenate(lifts, axis=0)


def pack_kernel(mass_h, velocity_h, weight_h, base_h, count_h, out, mass, velocity, weight, base, count, sems):
    pairs = ((count_h, count), (mass_h, mass), (base_h, base), (velocity_h, velocity), (weight_h, weight))
    copies = [pltpu.make_async_copy(a, b, sems.at[k]) for k, (a, b) in enumerate(pairs)]
    for copy in copies:
        copy.start()
    copies[0].wait()
    limit = jnp.broadcast_to(count[...], (GROUPS, CAP)).astype(F32).T
    slot = lax.broadcasted_iota(jnp.int32, (GROUPS, CAP), 1).astype(F32)
    live = jnp.where(slot < limit, 1.0, 0.0)
    copies[1].wait()
    out[pl.ds(ROW_M, GROUPS, stride=FIELDS), :] = mass[...] * live
    copies[2].wait()
    out[pl.ds(ROW_B, GROUPS, stride=FIELDS), :] = base[...].astype(F32)
    copies[3].wait()
    for axis in range(3):
        out[pl.ds(axis, GROUPS, stride=FIELDS), :] = velocity[axis]
    copies[4].wait()
    for corner in range(8):
        out[pl.ds(ROW_W + corner, GROUPS, stride=FIELDS), :] = weight[pl.ds(corner, GROUPS, stride=8), :]


def pack(*operands):
    return pl.pallas_call(
        pack_kernel,
        out_shape=shape(GROUPS * FIELDS, CAP),
        in_specs=[pl.BlockSpec(memory_space=pl.ANY)] * 5,
        out_specs=VM,
        scratch_shapes=[pltpu.VMEM(a.shape, a.dtype) for a in operands] + [pltpu.SemaphoreType.DMA((5,))],
        compiler_params=pltpu.CompilerParams(vmem_limit_bytes=67_000_000),
        name="pack",
    )(*operands)


def unpack_kernel(velocity, returned, out):
    for axis in range(3):
        out[axis] = FLIP * velocity[axis] + returned[pl.ds(axis, GROUPS, stride=3), :]


def unpack(velocity, returned):
    return pl.pallas_call(
        unpack_kernel,
        out_shape=shape(3, GROUPS, CAP),
        in_specs=[VM] * 2,
        out_specs=VM,
        compiler_params=SMALL,
        name="unpack",
    )(velocity, returned)


def spread_kernel(msg, density, water, out, plane_s, depth_s, value_s, left_a, hot_a, left_b, hot_b, acc):
    cells_of(msg, plane_s, depth_s)
    depth_s[...] = depth_s[...].astype(F32).T.astype(jnp.int32)
    mass = msg[pl.ds(ROW_M, GROUPS, stride=FIELDS), :]
    value_s[0] = mass
    for axis in range(3):
        value_s[1 + axis] = mass * msg[pl.ds(axis, GROUPS, stride=FIELDS), :]
    acc[...] = jnp.zeros_like(acc)
    level = lax.broadcasted_iota(jnp.int32, (CAP, DEPTH), 1)

    def build(chunk, left, hot):
        depths = pltpu.roll(depth_s[...], (GROUPS - chunk * CHUNK) % GROUPS, 1)
        for j in range(CHUNK):
            source = chunk * CHUNK + j
            columns = slice(j * CAP, (j + 1) * CAP)
            weights = tile_weights(msg, source, plane_s[pl.ds(source, 1), :])
            for f in range(4):
                value = weights * value_s[f, pl.ds(source, 1), :]
                left[f * 64 : (f + 1) * 64, columns] = value
                left[256 + f * 64 : 256 + (f + 1) * 64, columns] = remainder(value)
            hot[columns, :] = jnp.where(level == depths[:, j : j + 1], 1.0, 0.0)

    def multiply(left, hot):
        acc[...] += one_pass(left[...], hot[...])

    turns = GROUPS // CHUNK
    build(0, left_a, hot_a)

    def body(turn, carry):
        build(2 * turn + 1, left_b, hot_b)
        multiply(left_a, hot_a)
        build((2 * turn + 2) & (turns - 1), left_a, hot_a)
        multiply(left_b, hot_b)
        return carry

    lax.fori_loop(0, turns // 2, body, 0)
    grid = []
    for f in range(4):
        both = acc[f * 64 : (f + 1) * 64, :] + acc[256 + f * 64 : 256 + (f + 1) * 64, :]
        grid.append(both[:CELLS] + pltpu.roll(both[CELLS:], 1, 1))
    total = grid[0] + density[...]
    out[0] = total
    for axis in range(3):
        out[1 + axis] = (grid[1 + axis] + density[...] * water[axis]) / total


def spread(msg, density, water):
    left = pltpu.VMEM((512, CHUNK * CAP), F32)
    hot = pltpu.VMEM((CHUNK * CAP, DEPTH), F32)
    index = pltpu.VMEM((GROUPS, CAP), jnp.int32)
    return pl.pallas_call(
        spread_kernel,
        out_shape=shape(4, CELLS, DEPTH),
        in_specs=[VM] * 3,
        out_specs=VM,
        scratch_shapes=[index, index, pltpu.VMEM((4, GROUPS, CAP), F32)]
        + [left, hot, left, hot]
        + [pltpu.VMEM((512, DEPTH), F32)],
        compiler_params=PARAMS,
        name="spread",
    )(msg, density, water)


def next_x(row):
    return pltpu.roll(row, XE - 1, 0)


def prev_x(row):
    return pltpu.roll(row, 1, 0)


def next_z(row):
    return pltpu.roll(row, DEPTH - 1, 1)


def prev_z(row):
    return pltpu.roll(row, 1, 1)


def each_row(first, last, body, unroll=UNROLL):
    turns, rest = divmod(last - first, unroll)

    def step(turn, carry):
        for k in range(unroll):
            body(first + unroll * turn + k)
        return carry

    lax.fori_loop(0, turns, step, 0)
    for k in range(rest):
        body(last - rest + k)


def operate_row(field, y, offset, beta_x, beta_y, beta_z):
    here = field[y - offset]
    flux_x = beta_x[y] * (here - next_x(here))
    flux_z = beta_z[y] * (here - next_z(here))
    flux_y = beta_y[y] * (here - field[y - offset + 1])
    from_y = beta_y[y - 1] * (field[y - offset - 1] - here)
    return (
        DAMPING * here
        + (flux_x - prev_x(flux_x))
        + (flux_y - from_y)
        + (flux_z - prev_z(flux_z))
    )


def place(ext, corner, own, low_y, high_y, low_x, high_x, fix):
    for y in range(8):
        ext[HALO + y, 4:8, :] = own(slice(4 * y, 4 * y + 4))
    for y in range(HALO):
        rows = slice(4 * y, 4 * y + 4)
        ext[y, 4:8, :] = fix(low_y(rows), 1, 0)
        ext[HALO + 8 + y, 4:8, :] = fix(high_y(rows), 1, 2)
    for side, columns, source in ((0, slice(0, 4), low_x), (2, slice(8, 12), high_x)):
        for y in range(8):
            ext[HALO + y, columns, :] = fix(source(slice(4 * y, 4 * y + 4)), side, 1)
        for y in range(corner):
            first = CELLS + 4 * y
            ext[HALO - corner + y, columns, :] = fix(source(slice(first, first + 4)), side, 0)
            first = first + 4 * corner
            ext[HALO + 8 + y, columns, :] = fix(source(slice(first, first + 4)), side, 2)


def precondition(scaled, inverse, betas, update, first, second, finish, low, high, unroll=UNROLL):
    theta = (UPPER + LOWER) / 2.0
    delta = (UPPER - LOWER) / 2.0
    sigma = theta / delta

    def start(y):
        value = scaled[y] * (1.0 / theta)
        update[y] = value
        first[y] = value

    each_row(low, high, start, unroll)
    previous = 1.0 / sigma
    current = 1.0 / (2.0 * sigma - previous)

    def middle(y):
        misfit = scaled[y] - inverse[y] * operate_row(first, y, 0, *betas)
        value = current * previous * update[y] + (2.0 * current / delta) * misfit
        update[y] = value
        second[y] = first[y] + value

    each_row(low + 1, high - 1, middle, unroll)
    latest = 1.0 / (2.0 * sigma - current)

    def last(y):
        misfit = scaled[y] - inverse[y] * operate_row(second, y, 0, *betas)
        value = latest * current * update[y] + (2.0 * latest / delta) * misfit
        finish(y, second[y] + value)

    each_row(low + 2, high - 2, last, unroll)


def each_pair(base, body):
    def step(pair, carry):
        y = base + 2 * pair
        rows = pl.ds(pl.multiple_of(8 * pair, 8), 8)
        lower_half = lax.broadcasted_iota(jnp.int32, (8, DEPTH), 0) < 4
        for ref, first, second in zip(*body(y)):
            ref[rows, :] = jnp.where(lower_half, pltpu.roll(first[:8], 4, 0), second[:8])
        return carry

    lax.fori_loop(0, 4, step, 0)


def outside_fix(edge, infinite, value, column, row):
    outside = 0
    if column != 1:
        outside = outside + edge[0 if column == 0 else 1]
    if row != 1:
        outside = outside + edge[2 if row == 0 else 3]
    return jnp.where(outside > 0, infinite, value)


def face_row(total, y, end, cut, beta_x, beta_y, beta_z):
    here = total[y]
    across = 2.0 / (here + next_x(here))
    beta_x[y] = across if cut is None else jnp.where(cut, 0.0, across)
    beta_y[y] = 2.0 / (here + total[y + 1])
    beta_z[y] = jnp.where(end, 0.0, 2.0 / (here + next_z(here)))


def inverse_row(y, beta_x, beta_y, beta_z):
    across, along = beta_x[y], beta_z[y]
    return 1.0 / (
        DAMPING + across + prev_x(across) + beta_y[y] + beta_y[y - 1] + along + prev_z(along)
    )


def start_kernel(
    edge, own, low_y, high_y, low_x, high_x,
    basis, basis_own, image, scaled_own, source_own, total, up, down,
    ext, residual, scaled, beta_x, beta_y, beta_z, inverse, update, first, second,
):
    infinite = jnp.full((4, DEPTH), jnp.inf, F32)
    for f in range(4):
        target = ext.at[f - 1] if f else total
        empty = 0.0 if f else jnp.inf
        target[:, 12:16, :] = jnp.full((YE, 4, DEPTH), empty, F32)
        for y in range(HALO - CORNER):
            for row in (y, YE - 1 - y):
                target[row] = jnp.full((XE, DEPTH), empty, F32)

        def fix(value, column, row, f=f):
            return outside_fix(edge, infinite, value, column, row) if f == 0 else value

        place(
            target,
            CORNER,
            *[(lambda rows, ref=ref, f=f: ref[f, rows, :]) for ref in (own, low_y, high_y, low_x, high_x)],
            fix,
        )
    end = lax.broadcasted_iota(jnp.int32, (XE, DEPTH), 1) == DEPTH - 1
    betas = (beta_x, beta_y, beta_z)
    each_row(0, YE - 1, lambda y: face_row(total, y, end, None, *betas))

    def source(y):
        weight = inverse_row(y, *betas)
        inverse[y] = weight
        vx, vy, vz = ext[0, y], ext[1, y], ext[2, y]
        flow_x = beta_x[y] * (vx + next_x(vx))
        flow_z = beta_z[y] * (vz + next_z(vz))
        flow_y = beta_y[y] * (vy + ext[1, y + 1]) - beta_y[y - 1] * (ext[1, y - 1] + vy)
        value = -0.5 * ((flow_x - prev_x(flow_x)) + flow_y + (flow_z - prev_z(flow_z)))
        residual[y] = value
        scaled[y] = weight * value

    each_row(1, YE - 1, source)

    def finish(y, value):
        basis[y - 3] = value

    precondition(scaled, inverse, betas, update, first, second, finish, 1, YE - 1)

    def apply(y):
        value = operate_row(basis, y, 3, *betas)
        return value, basis[y - 3], residual[y], inverse[y] * value

    each_pair(HALO, lambda y: ((image, basis_own, source_own, scaled_own), apply(y), apply(y + 1)))
    up[:24, :] = scaled_own[8:, :]
    up[24:, :] = own[0, 8:16, :]
    down[:24, :] = scaled_own[:24, :]
    down[24:, :] = own[0, 16:24, :]


EXT = (YE, XE, DEPTH)
BROAD = (YW, XE, DEPTH)
BASIS = (10, XE, DEPTH)
BLOCK = (CELLS, DEPTH)


def start_solve(edge, own, near):
    return pl.pallas_call(
        start_kernel,
        out_shape=[shape(*BASIS)] + [shape(*BLOCK)] * 4 + [shape(*EXT)] + [shape(*BLOCK)] * 2,
        in_specs=[SM] + [VM] * 5,
        out_specs=[VM] * 8,
        scratch_shapes=[pltpu.VMEM((3,) + EXT, F32)] + [pltpu.VMEM(EXT, F32)] * 9,
        compiler_params=PARAMS,
        name="start_solve",
    )(edge, own, *near)


def four(index):
    return slice(4 * index, 4 * index + 4)


def two(index):
    return slice(2 * index, 2 * index + 2)


def solve_kernel(
    edge, total_near, scaled_own, wide_ly, wide_hy, wide_lx, wide_hx, far_lx, far_hx,
    basis_0, own_0, image_0, source_own,
    basis_1, basis_2, out_x, out_y, out_z, sums,
    total, scaled, beta_x, beta_y, beta_z, inverse, update, first, second, vector, scaled_1, vector_2,
    own_1, image_1, own_2, image_2,
):
    infinite = jnp.full((4, DEPTH), jnp.inf, F32)
    for y in range(YE):
        total[y + 2] = total_near[y]
    for y in range(YW):
        if y < 2 or y >= YW - 2:
            total[y] = jnp.full((XE, DEPTH), jnp.inf, F32)
        scaled[y] = jnp.zeros((XE, DEPTH), F32)

    def put(y, columns, value, column):
        row = 0 if y < WIDE else 2
        total[y, columns, :] = outside_fix(edge, infinite, value, column, row)

    middle = slice(4, 8)
    for y in range(8):
        scaled[WIDE + y, middle, :] = scaled_own[four(y), :]
    for y in range(WIDE):
        scaled[y, middle, :] = wide_ly[four(y), :]
        scaled[WIDE + 8 + y, middle, :] = wide_hy[four(y), :]
    for y in range(2):
        put(y, middle, wide_ly[four(WIDE + y), :], 1)
        put(WIDE + 12 + y, middle, wide_hy[four(WIDE + y), :], 1)
    for side, columns, wide in ((0, slice(0, 4), wide_lx), (2, slice(8, 12), wide_hx)):
        for y in range(8):
            scaled[WIDE + y, columns, :] = wide[four(y), :]
        for y in range(5):
            scaled[1 + y, columns, :] = wide[four(8 + y), :]
            scaled[WIDE + 8 + y, columns, :] = wide[four(13 + y), :]
        for place_in, y in enumerate((1, 2, WIDE + 11, WIDE + 12)):
            put(y, columns, wide[four(18 + place_in), :], side)
    for flag, columns, far in ((4, slice(14, 16), far_lx), (5, slice(12, 14), far_hx)):
        for y in range(10):
            row = 0 if y == 0 else (2 if y == 9 else 1)
            outside = edge[flag]
            if row != 1:
                outside = outside + edge[2 if row == 0 else 3]
            value = far[two(10 + y), :]
            total[WIDE - 1 + y, columns, :] = jnp.where(outside > 0, infinite[:2], value)
            scaled[WIDE - 1 + y, columns, :] = far[two(y), :]

    end = lax.broadcasted_iota(jnp.int32, (XE, DEPTH), 1) == DEPTH - 1
    cut = lax.broadcasted_iota(jnp.int32, (XE, DEPTH), 0) == 13
    betas = (beta_x, beta_y, beta_z)
    each_row(0, YW - 1, lambda y: face_row(total, y, end, cut, *betas), 8)

    def invert(y):
        inverse[y] = inverse_row(y, *betas)

    each_row(1, YW - 1, invert, 8)

    def finish_1(y, value):
        vector[y] = value

    precondition(scaled, inverse, betas, update, first, second, finish_1, 0, YW, 8)

    def rescale(y):
        value = operate_row(vector, y, 0, *betas)
        second[y] = value
        scaled_1[y] = inverse[y] * value

    each_row(3, YW - 3, rescale, 8)
    each_pair(WIDE, lambda y: ((own_1, image_1), (vector[y], second[y]), (vector[y + 1], second[y + 1])))

    def finish_2(y, value):
        before = basis_0[y - 5]
        vector_2[y - 5] = value
        basis_1[y - 5] = before - vector[y]
        basis_2[y - 5] = (before - vector[y]) - (vector[y] - value)
        out_x[y - 5] = beta_x[y]
        out_y[y - 5] = beta_y[y]
        out_z[y - 5] = beta_z[y]

    precondition(scaled_1, inverse, betas, update, first, second, finish_2, 3, YW - 3, 8)

    def apply(y):
        return vector_2[y - 5], operate_row(vector_2, y, 5, *betas)

    each_pair(WIDE, lambda y: ((own_2, image_2), apply(y), apply(y + 1)))
    v0, v1, v2 = own_0[...], own_1[...], own_2[...]
    a0, a1, a2 = image_0[...], image_1[...], image_2[...]
    vectors = (v0, v0 - v1, (v0 - v1) - (v1 - v2))
    images = (a0, a0 - a1, (a0 - a1) - (a1 - a2))
    source = source_own[...]
    pairs = [(vectors[i], images[j]) for i in range(3) for j in range(i, 3)]
    pairs += [(item, source) for item in vectors]
    lane = lax.broadcasted_iota(jnp.int32, (1, CAP), 1)
    row = jnp.zeros((1, CAP), F32)
    for place_in, (a, b) in enumerate(pairs):
        folded = jnp.sum((a * b).reshape(4, 8, DEPTH), axis=0)
        folded = (folded[:, :128] + folded[:, 128:256]) + (folded[:, 256:384] + folded[:, 384:])
        row = jnp.where(lane == place_in, jnp.sum(folded, keepdims=True), row)
    sums[...] = jnp.broadcast_to(row, (GROUPS, CAP))


def widen_kernel(block, low_y, high_y, total, column, far_up, far_down):
    column[:32, :] = block[...]
    column[32:52, :] = low_y[4:24, :]
    column[52:72, :] = high_y[:20, :]
    column[72:76, :] = low_y[28:32, :]
    column[76:80, :] = total[0, 4:8, :]
    column[80:84, :] = total[YE - 1, 4:8, :]
    column[84:88, :] = high_y[24:28, :]
    for first, target in ((2, far_up), (0, far_down)):
        target[two(0), :] = low_y[20 + first : 22 + first, :]
        for y in range(8):
            target[two(1 + y), :] = block[4 * y + first : 4 * y + first + 2, :]
        target[two(9), :] = high_y[first : first + 2, :]
        for y in range(10):
            target[two(10 + y), :] = total[HALO - 1 + y, 4 + first : 6 + first, :]


def widen(block, low_y, high_y, total):
    return pl.pallas_call(
        widen_kernel,
        out_shape=[shape(88, DEPTH), shape(40, DEPTH), shape(40, DEPTH)],
        in_specs=[VM] * 4,
        out_specs=[VM] * 3,
        compiler_params=SMALL,
        name="widen",
    )(block, low_y, high_y, total)


def solve(edge, total, scaled, wide, basis_0, *inner):
    return pl.pallas_call(
        solve_kernel,
        out_shape=[shape(*BASIS)] * 5 + [shape(GROUPS, CAP)],
        in_specs=[SM] + [VM] * 12,
        out_specs=[VM] * 6,
        scratch_shapes=[pltpu.VMEM(BROAD, F32)] * 11
        + [pltpu.VMEM(BASIS, F32)]
        + [pltpu.VMEM(BLOCK, F32)] * 4,
        compiler_params=PARAMS,
        name="solve",
    )(edge, total, scaled, *wide, basis_0, *inner)


def coefficients(sums):
    total = jnp.sum(sums[...], axis=0, keepdims=True)
    g00, g01, g02, g11, g12, g22, b0, b1, b2 = [total[:, k : k + 1] for k in range(9)]
    l1 = g01 / g00
    l2 = g02 / g00
    d1 = g11 - l1 * g01
    keep_1 = d1 > 1e-7 * g11
    d1 = jnp.where(keep_1, d1, 1.0)
    m = jnp.where(keep_1, (g12 - l2 * g01) / d1, 0.0)
    d2 = g22 - l2 * g02 - m * m * d1
    keep_2 = d2 > 1e-7 * g22
    d2 = jnp.where(keep_2, d2, 1.0)
    y1 = b1 - l1 * b0
    y2 = b2 - l2 * b0 - m * y1
    c2 = jnp.where(keep_2, y2 / d2, 0.0)
    c1 = jnp.where(keep_1, y1 / d1, 0.0) - m * c2
    c0 = b0 / g00 - l1 * c1 - l2 * c2
    return c0, c1, c2


def gather_kernel(
    sums, basis_0, basis_1, basis_2, beta_x, beta_y, beta_z, own, msg,
    out, pressure_out, plane_s, depth_s, pressure, carried, table_s, hot_a, hot_b,
):
    c0, c1, c2 = [jnp.broadcast_to(c, (XE, DEPTH)) for c in coefficients(sums)]

    def combine(y):
        pressure[y] = c0 * basis_0[y] + c1 * basis_1[y] + c2 * basis_2[y]

    each_row(0, 10, combine)

    def slopes(y):
        here = pressure[y]
        flux_x = beta_x[y] * (here - next_x(here))
        flux_z = beta_z[y] * (here - next_z(here))
        flux_y = beta_y[y] * (here - pressure[y + 1])
        from_y = beta_y[y - 1] * (pressure[y - 1] - here)
        return (
            (flux_x + prev_x(flux_x)) * 0.5,
            (flux_y + from_y) * 0.5,
            (flux_z + prev_z(flux_z)) * 0.5,
            here,
        )

    targets = (carried.at[0], carried.at[1], carried.at[2], pressure_out)
    each_pair(1, lambda y: (targets, slopes(y), slopes(y + 1)))
    for axis in range(3):
        velocity = own[1 + axis]
        value = (velocity + carried[axis]) - FLIP * velocity
        for lift, level in ((0, value), (1, next_z(value))):
            first = axis * 64 + lift * CELLS
            table_s[first : first + CELLS, :] = level
            table_s[192 + first : 192 + first + CELLS, :] = remainder(level)
    cells_of(msg, plane_s, depth_s)
    level = lax.broadcasted_iota(jnp.int32, (DEPTH, CAP), 0)

    def build(chunk, hot):
        for j in range(PICK):
            depth_row = depth_s[pl.ds(chunk * PICK + j, 1), :]
            hot[:, j * CAP : (j + 1) * CAP] = jnp.where(level == depth_row, 1.0, 0.0)

    def pick(chunk, hot):
        both = one_pass(table_s[...], hot[...])
        table = both[:192] + both[192:]
        for j in range(PICK):
            source = chunk * PICK + j
            weights = tile_weights(msg, source, plane_s[pl.ds(source, 1), :])
            for axis in range(3):
                picked = table[axis * 64 : (axis + 1) * 64, j * CAP : (j + 1) * CAP] * weights
                out[pl.ds(3 * source + axis, 1), :] = jnp.sum(picked, axis=0, keepdims=True)

    turns = GROUPS // PICK
    build(0, hot_a)

    def body(turn, carry):
        build(2 * turn + 1, hot_b)
        pick(2 * turn, hot_a)
        build((2 * turn + 2) & (turns - 1), hot_a)
        pick(2 * turn + 1, hot_b)
        return carry

    lax.fori_loop(0, turns // 2, body, 0)


def gather(sums, bases, betas, own, msg):
    index = pltpu.VMEM((GROUPS, CAP), jnp.int32)
    hot = pltpu.VMEM((DEPTH, PICK * CAP), F32)
    return pl.pallas_call(
        gather_kernel,
        out_shape=[shape(3 * GROUPS, CAP), shape(*BLOCK)],
        in_specs=[VM] * 9,
        out_specs=[VM] * 2,
        scratch_shapes=[index, index, pltpu.VMEM(BASIS, F32), pltpu.VMEM((3,) + BLOCK, F32), pltpu.VMEM((384, DEPTH), F32), hot, hot],
        compiler_params=LARGE,
        name="gather",
    )(sums, *bases, *betas, own, msg)


def exchange(block, n_x, n_y, corner):
    up_x = [(i, (i + 1) % n_x) for i in range(n_x)]
    up_y = [(i, (i + 1) % n_y) for i in range(n_y)]
    down_x, down_y = [[(b, a) for a, b in up] for up in (up_x, up_y)]
    half = 4 * HALO
    low_y = lax.ppermute(block[..., CELLS - half :, :], "yz", up_y)
    high_y = lax.ppermute(block[..., :half, :], "yz", down_y)
    near = 4 * corner
    near_low, near_high = low_y, high_y
    if corner < HALO:
        near_low, near_high = low_y[..., half - near :, :], high_y[..., :near, :]
    column = jnp.concatenate([block, near_low, near_high], axis=-2)
    return low_y, high_y, lax.ppermute(column, "gx", up_x), lax.ppermute(column, "gx", down_x)


def exchange_wide(block, up, down, total, n_x, n_y):
    up_x, up_xx = [[(i, (i + k) % n_x) for i in range(n_x)] for k in (1, 2)]
    up_y = [(i, (i + 1) % n_y) for i in range(n_y)]
    down_x, down_xx, down_y = [[(b, a) for a, b in pairs] for pairs in (up_x, up_xx, up_y)]
    low_y = lax.ppermute(up, "yz", up_y)
    high_y = lax.ppermute(down, "yz", down_y)
    column, far_up, far_down = widen(block, low_y, high_y, total)
    far_lx = lax.ppermute(far_up, "gx", up_xx)
    far_hx = lax.ppermute(far_down, "gx", down_xx)
    low_x = lax.ppermute(column, "gx", up_x)
    high_x = lax.ppermute(column, "gx", down_x)
    return low_y, high_y, low_x, high_x, far_lx, far_hx


def by_block(field):
    turned = jnp.swapaxes(field, -3, -2)
    return turned.reshape(turned.shape[:-3] + (CELLS, DEPTH))


def local(part_mass, part_vel, corner_weight, corner_base, slot_counts, water_vel, solid_flag):
    n_x, n_y = lax.axis_size("gx"), lax.axis_size("yz")
    at_x, at_y = lax.axis_index("gx"), lax.axis_index("yz")
    edge = jnp.stack(
        [at_x == 0, at_x == n_x - 1, at_y == 0, at_y == n_y - 1, at_x <= 1, at_x >= n_x - 2]
    ).astype(jnp.int32)
    velocity = jnp.swapaxes(part_vel[0], 0, 1)
    message = pack(
        part_mass[0], velocity, corner_weight.reshape(8 * GROUPS, CAP), corner_base[0], slot_counts
    )
    msg = lax.all_to_all(message.reshape(GROUPS, 1, FIELDS * CAP), ALL, 0, 0, tiled=True)
    msg = msg.reshape(GROUPS * FIELDS, CAP)
    density = by_block(jnp.where(solid_flag == 1, SOLID_WATER, 1.0).astype(F32))
    own = spread(msg, density, by_block(water_vel))
    near = exchange(own, n_x, n_y, CORNER)
    basis_0, own_0, image_0, scaled, source, total, up, down = start_solve(edge, own, near)
    wide = exchange_wide(scaled, up, down, total, n_x, n_y)
    basis_1, basis_2, *betas, sums = solve(
        edge, total, scaled, wide, basis_0, own_0, image_0, source
    )
    sums = lax.all_to_all(sums, ALL, 0, 0, tiled=True)
    sampled, pressure = gather(sums, (basis_0, basis_1, basis_2), betas, own, msg)
    returned = lax.all_to_all(sampled.reshape(GROUPS, 1, 3 * CAP), ALL, 0, 0, tiled=True)
    final = unpack(velocity, returned.reshape(3 * GROUPS, CAP))
    pressure = jnp.swapaxes(pressure.reshape(8, 4, DEPTH), 0, 1)
    return jnp.swapaxes(final, 0, 1)[None], pressure


def solution(mesh):
    parts = P(ALL, None, None)
    in_specs = (parts, P(ALL, None, None, None), P(ALL, None, None, None), parts, P(ALL, None), P(None, "gx", "yz", None), P("gx", "yz", None))
    out_specs = (P(ALL, None, None, None), P("gx", "yz", None))
    return jax.shard_map(local, mesh=mesh, in_specs=in_specs, out_specs=out_specs, check_vma=False)
```

```python
import jax
import jax.numpy as jnp
from jax import lax
from jax.experimental import pallas as pl
from jax.experimental.pallas import tpu as pltpu
from jax.sharding import PartitionSpec as P

ALL = ("gx", "yz")
DAMPING = 0.05
SOLID_WATER = 0.1
FLIP = 0.9
LOWER = 0.1
UPPER = 2.0
DEGREE = 3
GROUPS = 128
CAP = 128
FIELDS = 13
ROW_W = 3
ROW_M = 11
ROW_B = 12
CELLS = 32
DEPTH = 512
CHUNK = 8
PICK = 16
HALO = 4
UNROLL = 4
WIDE = 6
YW = 8 + 2 * WIDE
CORNER = 3
YE = 8 + 2 * HALO
XE = 16
PARAMS = pltpu.CompilerParams(vmem_limit_bytes=20 * 1024 * 1024)
LARGE = pltpu.CompilerParams(vmem_limit_bytes=28 * 1024 * 1024)
SMALL = pltpu.CompilerParams(vmem_limit_bytes=8 * 1024 * 1024)
VM = pl.BlockSpec(memory_space=pltpu.VMEM)
SM = pl.BlockSpec(memory_space=pltpu.SMEM)
F32 = jnp.float32
BF16 = jnp.bfloat16


def shape(*dims):
    return jax.ShapeDtypeStruct(dims, F32)


def remainder(value):
    return value - value.astype(BF16).astype(F32)


def one_pass(left, right):
    return lax.dot_general(
        left, right, (((1,), (0,)), ((), ())), precision=lax.Precision.DEFAULT, preferred_element_type=F32
    )


def cells_of(msg, plane_s, depth_s):
    base = msg[pl.ds(ROW_B, GROUPS, stride=FIELDS), :].astype(jnp.int32)
    plane = base >> 9
    plane_s[...] = (plane & 7) * 4 + (plane >> 3)
    depth_s[...] = base & 511


def tile_weights(msg, source, plane_row):
    away = lax.broadcasted_iota(jnp.int32, (CELLS, CAP), 0) - plane_row
    here, next_y, next_x, next_xy = away == 0, away == 4, away == 1, away == 5
    zero = jnp.zeros((CELLS, CAP), F32)

    def weight(corner):
        row = msg[pl.ds(FIELDS * source + ROW_W + corner, 1), :]
        return jnp.broadcast_to(row, (CELLS, CAP))

    lifts = []
    for lift in (0, 1):
        value = jnp.where(next_xy, weight(6 + lift), zero)
        value = jnp.where(next_x, weight(4 + lift), value)
        value = jnp.where(next_y, weight(2 + lift), value)
        lifts.append(jnp.where(here, weight(lift), value))
    return jnp.concatenate(lifts, axis=0)


def pack_kernel(mass_h, velocity_h, weight_h, base_h, count_h, out, mass, velocity, weight, base, count, sems):
    pairs = ((count_h, count), (mass_h, mass), (base_h, base), (velocity_h, velocity), (weight_h, weight))
    copies = [pltpu.make_async_copy(a, b, sems.at[k]) for k, (a, b) in enumerate(pairs)]
    for copy in copies:
        copy.start()
    copies[0].wait()
    limit = jnp.broadcast_to(count[...], (GROUPS, CAP)).astype(F32).T
    slot = lax.broadcasted_iota(jnp.int32, (GROUPS, CAP), 1).astype(F32)
    live = jnp.where(slot < limit, 1.0, 0.0)
    copies[1].wait()
    out[pl.ds(ROW_M, GROUPS, stride=FIELDS), :] = mass[...] * live
    copies[2].wait()
    out[pl.ds(ROW_B, GROUPS, stride=FIELDS), :] = base[...].astype(F32)
    copies[3].wait()
    for axis in range(3):
        out[pl.ds(axis, GROUPS, stride=FIELDS), :] = velocity[axis]
    copies[4].wait()
    for corner in range(8):
        out[pl.ds(ROW_W + corner, GROUPS, stride=FIELDS), :] = weight[pl.ds(corner, GROUPS, stride=8), :]


def pack(*operands):
    return pl.pallas_call(
        pack_kernel,
        out_shape=shape(GROUPS * FIELDS, CAP),
        in_specs=[pl.BlockSpec(memory_space=pl.ANY)] * 5,
        out_specs=VM,
        scratch_shapes=[pltpu.VMEM(a.shape, a.dtype) for a in operands] + [pltpu.SemaphoreType.DMA((5,))],
        compiler_params=pltpu.CompilerParams(vmem_limit_bytes=67_000_000),
        name="pack",
    )(*operands)


def unpack_kernel(velocity, returned, out):
    for axis in range(3):
        out[axis] = FLIP * velocity[axis] + returned[pl.ds(axis, GROUPS, stride=3), :]


def unpack(velocity, returned):
    return pl.pallas_call(
        unpack_kernel,
        out_shape=shape(3, GROUPS, CAP),
        in_specs=[VM] * 2,
        out_specs=VM,
        compiler_params=SMALL,
        name="unpack",
    )(velocity, returned)


def spread_kernel(msg, density, water, out, up, down, plane_s, depth_s, value_s, left_a, hot_a, left_b, hot_b, acc):
    cells_of(msg, plane_s, depth_s)
    depth_s[...] = depth_s[...].astype(F32).T.astype(jnp.int32)
    mass = msg[pl.ds(ROW_M, GROUPS, stride=FIELDS), :]
    value_s[0] = mass
    for axis in range(3):
        value_s[1 + axis] = mass * msg[pl.ds(axis, GROUPS, stride=FIELDS), :]
    acc[...] = jnp.zeros_like(acc)
    level = lax.broadcasted_iota(jnp.int32, (CAP, DEPTH), 1)

    def build(chunk, left, hot):
        depths = pltpu.roll(depth_s[...], (GROUPS - chunk * CHUNK) % GROUPS, 1)
        for j in range(CHUNK):
            source = chunk * CHUNK + j
            columns = slice(j * CAP, (j + 1) * CAP)
            weights = tile_weights(msg, source, plane_s[pl.ds(source, 1), :])
            for f in range(4):
                value = weights * value_s[f, pl.ds(source, 1), :]
                left[f * 64 : (f + 1) * 64, columns] = value
                left[256 + f * 64 : 256 + (f + 1) * 64, columns] = remainder(value)
            hot[columns, :] = jnp.where(level == depths[:, j : j + 1], 1.0, 0.0)

    def multiply(left, hot):
        acc[...] += one_pass(left[...], hot[...])

    turns = GROUPS // CHUNK
    build(0, left_a, hot_a)

    def body(turn, carry):
        build(2 * turn + 1, left_b, hot_b)
        multiply(left_a, hot_a)
        build((2 * turn + 2) & (turns - 1), left_a, hot_a)
        multiply(left_b, hot_b)
        return carry

    lax.fori_loop(0, turns // 2, body, 0)
    grid = []
    for f in range(4):
        both = acc[f * 64 : (f + 1) * 64, :] + acc[256 + f * 64 : 256 + (f + 1) * 64, :]
        grid.append(both[:CELLS] + pltpu.roll(both[CELLS:], 1, 1))
    total = grid[0] + density[...]
    values = [total] + [(grid[1 + axis] + density[...] * water[axis]) / total for axis in range(3)]
    for f, value in enumerate(values):
        out[f] = value
        up[f] = value[CELLS // 2 :]
        down[f] = value[: CELLS // 2]


def spread(msg, density, water):
    left = pltpu.VMEM((512, CHUNK * CAP), F32)
    hot = pltpu.VMEM((CHUNK * CAP, DEPTH), F32)
    index = pltpu.VMEM((GROUPS, CAP), jnp.int32)
    return pl.pallas_call(
        spread_kernel,
        out_shape=[shape(4, CELLS, DEPTH)] + [shape(4, CELLS // 2, DEPTH)] * 2,
        in_specs=[VM] * 3,
        out_specs=[VM] * 3,
        scratch_shapes=[index, index, pltpu.VMEM((4, GROUPS, CAP), F32)]
        + [left, hot, left, hot]
        + [pltpu.VMEM((512, DEPTH), F32)],
        compiler_params=PARAMS,
        name="spread",
    )(msg, density, water)


def next_x(row):
    return pltpu.roll(row, XE - 1, 0)


def prev_x(row):
    return pltpu.roll(row, 1, 0)


def next_z(row):
    return pltpu.roll(row, DEPTH - 1, 1)


def prev_z(row):
    return pltpu.roll(row, 1, 1)


def each_row(first, last, body, unroll=UNROLL):
    turns, rest = divmod(last - first, unroll)

    def step(turn, carry):
        for k in range(unroll):
            body(first + unroll * turn + k)
        return carry

    lax.fori_loop(0, turns, step, 0)
    for k in range(rest):
        body(last - rest + k)


def operate_row(field, y, offset, beta_x, beta_y, beta_z):
    here = field[y - offset]
    flux_x = beta_x[y] * (here - next_x(here))
    flux_z = beta_z[y] * (here - next_z(here))
    flux_y = beta_y[y] * (here - field[y - offset + 1])
    from_y = beta_y[y - 1] * (field[y - offset - 1] - here)
    return (
        DAMPING * here
        + (flux_x - prev_x(flux_x))
        + (flux_y - from_y)
        + (flux_z - prev_z(flux_z))
    )


def place(ext, corner, own, low_y, high_y, low_x, high_x, fix):
    for y in range(8):
        ext[HALO + y, 4:8, :] = own(slice(4 * y, 4 * y + 4))
    for y in range(HALO):
        rows = slice(4 * y, 4 * y + 4)
        ext[y, 4:8, :] = fix(low_y(rows), 1, 0)
        ext[HALO + 8 + y, 4:8, :] = fix(high_y(rows), 1, 2)
    for side, columns, source in ((0, slice(0, 4), low_x), (2, slice(8, 12), high_x)):
        for y in range(8):
            ext[HALO + y, columns, :] = fix(source(slice(4 * y, 4 * y + 4)), side, 1)
        for y in range(corner):
            first = CELLS + 4 * y
            ext[HALO - corner + y, columns, :] = fix(source(slice(first, first + 4)), side, 0)
            first = first + 4 * corner
            ext[HALO + 8 + y, columns, :] = fix(source(slice(first, first + 4)), side, 2)


def precondition(scaled, inverse, betas, update, first, second, finish, low, high, unroll=UNROLL):
    theta = (UPPER + LOWER) / 2.0
    delta = (UPPER - LOWER) / 2.0
    sigma = theta / delta

    def start(y):
        value = scaled[y] * (1.0 / theta)
        update[y] = value
        first[y] = value

    each_row(low, high, start, unroll)
    previous = 1.0 / sigma
    current = 1.0 / (2.0 * sigma - previous)

    def middle(y):
        misfit = scaled[y] - inverse[y] * operate_row(first, y, 0, *betas)
        value = current * previous * update[y] + (2.0 * current / delta) * misfit
        update[y] = value
        second[y] = first[y] + value

    each_row(low + 1, high - 1, middle, unroll)
    latest = 1.0 / (2.0 * sigma - current)

    def last(y):
        misfit = scaled[y] - inverse[y] * operate_row(second, y, 0, *betas)
        value = latest * current * update[y] + (2.0 * latest / delta) * misfit
        finish(y, second[y] + value)

    each_row(low + 2, high - 2, last, unroll)


def each_pair(base, body):
    def step(pair, carry):
        y = base + 2 * pair
        rows = pl.ds(pl.multiple_of(8 * pair, 8), 8)
        lower_half = lax.broadcasted_iota(jnp.int32, (8, DEPTH), 0) < 4
        for ref, first, second in zip(*body(y)):
            ref[rows, :] = jnp.where(lower_half, pltpu.roll(first[:8], 4, 0), second[:8])
        return carry

    lax.fori_loop(0, 4, step, 0)


def outside_fix(edge, infinite, value, column, row):
    outside = 0
    if column != 1:
        outside = outside + edge[0 if column == 0 else 1]
    if row != 1:
        outside = outside + edge[2 if row == 0 else 3]
    return jnp.where(outside > 0, infinite, value)


def face_row(total, y, end, cut, beta_x, beta_y, beta_z):
    here = total[y]
    across = 2.0 / (here + next_x(here))
    beta_x[y] = across if cut is None else jnp.where(cut, 0.0, across)
    beta_y[y] = 2.0 / (here + total[y + 1])
    beta_z[y] = jnp.where(end, 0.0, 2.0 / (here + next_z(here)))


def inverse_row(y, beta_x, beta_y, beta_z):
    across, along = beta_x[y], beta_z[y]
    return 1.0 / (
        DAMPING + across + prev_x(across) + beta_y[y] + beta_y[y - 1] + along + prev_z(along)
    )


def start_kernel(
    edge, own, low_y, high_y, low_x, high_x,
    basis, basis_own, image, scaled_own, source_own, total, up, down,
    ext, residual, scaled, beta_x, beta_y, beta_z, inverse, update, first, second,
):
    infinite = jnp.full((4, DEPTH), jnp.inf, F32)
    for f in range(4):
        target = ext.at[f - 1] if f else total
        empty = 0.0 if f else jnp.inf
        target[:, 12:16, :] = jnp.full((YE, 4, DEPTH), empty, F32)
        for y in range(HALO - CORNER):
            for row in (y, YE - 1 - y):
                target[row] = jnp.full((XE, DEPTH), empty, F32)

        def fix(value, column, row, f=f):
            return outside_fix(edge, infinite, value, column, row) if f == 0 else value

        place(
            target,
            CORNER,
            *[(lambda rows, ref=ref, f=f: ref[f, rows, :]) for ref in (own, low_y, high_y, low_x, high_x)],
            fix,
        )
    end = lax.broadcasted_iota(jnp.int32, (XE, DEPTH), 1) == DEPTH - 1
    betas = (beta_x, beta_y, beta_z)
    each_row(0, YE - 1, lambda y: face_row(total, y, end, None, *betas))

    def source(y):
        weight = inverse_row(y, *betas)
        inverse[y] = weight
        vx, vy, vz = ext[0, y], ext[1, y], ext[2, y]
        flow_x = beta_x[y] * (vx + next_x(vx))
        flow_z = beta_z[y] * (vz + next_z(vz))
        flow_y = beta_y[y] * (vy + ext[1, y + 1]) - beta_y[y - 1] * (ext[1, y - 1] + vy)
        value = -0.5 * ((flow_x - prev_x(flow_x)) + flow_y + (flow_z - prev_z(flow_z)))
        residual[y] = value
        scaled[y] = weight * value

    each_row(1, YE - 1, source)

    def finish(y, value):
        basis[y - 3] = value

    precondition(scaled, inverse, betas, update, first, second, finish, 1, YE - 1)

    def apply(y):
        value = operate_row(basis, y, 3, *betas)
        return value, basis[y - 3], residual[y], inverse[y] * value

    each_pair(HALO, lambda y: ((image, basis_own, source_own, scaled_own), apply(y), apply(y + 1)))
    up[:24, :] = scaled_own[8:, :]
    up[24:, :] = own[0, 8:16, :]
    down[:24, :] = scaled_own[:24, :]
    down[24:, :] = own[0, 16:24, :]


EXT = (YE, XE, DEPTH)
BROAD = (YW, XE, DEPTH)
BASIS = (10, XE, DEPTH)
BLOCK = (CELLS, DEPTH)


def start_solve(edge, own, near):
    return pl.pallas_call(
        start_kernel,
        out_shape=[shape(*BASIS)] + [shape(*BLOCK)] * 4 + [shape(*EXT)] + [shape(*BLOCK)] * 2,
        in_specs=[SM] + [VM] * 5,
        out_specs=[VM] * 8,
        scratch_shapes=[pltpu.VMEM((3,) + EXT, F32)] + [pltpu.VMEM(EXT, F32)] * 9,
        compiler_params=PARAMS,
        name="start_solve",
    )(edge, own, *near)


def four(index):
    return slice(4 * index, 4 * index + 4)


def two(index):
    return slice(2 * index, 2 * index + 2)


def solve_kernel(
    edge, total_near, scaled_own, wide_ly, wide_hy, wide_lx, wide_hx, far_lx, far_hx,
    basis_0, own_0, image_0, source_own,
    basis_1, basis_2, out_x, out_y, out_z, sums,
    total, scaled, beta_x, beta_y, beta_z, inverse, update, first, second, vector, scaled_1, vector_2,
    own_1, image_1, own_2, image_2,
):
    infinite = jnp.full((4, DEPTH), jnp.inf, F32)
    for y in range(YE):
        total[y + 2] = total_near[y]
    for y in range(YW):
        if y < 2 or y >= YW - 2:
            total[y] = jnp.full((XE, DEPTH), jnp.inf, F32)
        scaled[y] = jnp.zeros((XE, DEPTH), F32)

    def put(y, columns, value, column):
        row = 0 if y < WIDE else 2
        total[y, columns, :] = outside_fix(edge, infinite, value, column, row)

    middle = slice(4, 8)
    for y in range(8):
        scaled[WIDE + y, middle, :] = scaled_own[four(y), :]
    for y in range(WIDE):
        scaled[y, middle, :] = wide_ly[four(y), :]
        scaled[WIDE + 8 + y, middle, :] = wide_hy[four(y), :]
    for y in range(2):
        put(y, middle, wide_ly[four(WIDE + y), :], 1)
        put(WIDE + 12 + y, middle, wide_hy[four(WIDE + y), :], 1)
    for side, columns, wide in ((0, slice(0, 4), wide_lx), (2, slice(8, 12), wide_hx)):
        for y in range(8):
            scaled[WIDE + y, columns, :] = wide[four(y), :]
        for y in range(5):
            scaled[1 + y, columns, :] = wide[four(8 + y), :]
            scaled[WIDE + 8 + y, columns, :] = wide[four(13 + y), :]
        for place_in, y in enumerate((1, 2, WIDE + 11, WIDE + 12)):
            put(y, columns, wide[four(18 + place_in), :], side)
    for flag, columns, far in ((4, slice(14, 16), far_lx), (5, slice(12, 14), far_hx)):
        for y in range(10):
            row = 0 if y == 0 else (2 if y == 9 else 1)
            outside = edge[flag]
            if row != 1:
                outside = outside + edge[2 if row == 0 else 3]
            value = far[two(10 + y), :]
            total[WIDE - 1 + y, columns, :] = jnp.where(outside > 0, infinite[:2], value)
            scaled[WIDE - 1 + y, columns, :] = far[two(y), :]

    end = lax.broadcasted_iota(jnp.int32, (XE, DEPTH), 1) == DEPTH - 1
    cut = lax.broadcasted_iota(jnp.int32, (XE, DEPTH), 0) == 13
    betas = (beta_x, beta_y, beta_z)
    each_row(0, YW - 1, lambda y: face_row(total, y, end, cut, *betas), 8)

    def invert(y):
        inverse[y] = inverse_row(y, *betas)

    each_row(1, YW - 1, invert, 8)

    def finish_1(y, value):
        vector[y] = value

    precondition(scaled, inverse, betas, update, first, second, finish_1, 0, YW, 8)

    def rescale(y):
        value = operate_row(vector, y, 0, *betas)
        second[y] = value
        scaled_1[y] = inverse[y] * value

    each_row(3, YW - 3, rescale, 8)
    each_pair(WIDE, lambda y: ((own_1, image_1), (vector[y], second[y]), (vector[y + 1], second[y + 1])))

    def finish_2(y, value):
        before = basis_0[y - 5]
        vector_2[y - 5] = value
        basis_1[y - 5] = before - vector[y]
        basis_2[y - 5] = (before - vector[y]) - (vector[y] - value)
        out_x[y - 5] = beta_x[y]
        out_y[y - 5] = beta_y[y]
        out_z[y - 5] = beta_z[y]

    precondition(scaled_1, inverse, betas, update, first, second, finish_2, 3, YW - 3, 8)

    def apply(y):
        return vector_2[y - 5], operate_row(vector_2, y, 5, *betas)

    each_pair(WIDE, lambda y: ((own_2, image_2), apply(y), apply(y + 1)))
    v0, v1, v2 = own_0[...], own_1[...], own_2[...]
    a0, a1, a2 = image_0[...], image_1[...], image_2[...]
    vectors = (v0, v0 - v1, (v0 - v1) - (v1 - v2))
    images = (a0, a0 - a1, (a0 - a1) - (a1 - a2))
    source = source_own[...]
    pairs = [(vectors[i], images[j]) for i in range(3) for j in range(i, 3)]
    pairs += [(item, source) for item in vectors]
    lane = lax.broadcasted_iota(jnp.int32, (1, CAP), 1)
    row = jnp.zeros((1, CAP), F32)
    for place_in, (a, b) in enumerate(pairs):
        folded = jnp.sum((a * b).reshape(4, 8, DEPTH), axis=0)
        folded = (folded[:, :128] + folded[:, 128:256]) + (folded[:, 256:384] + folded[:, 384:])
        row = jnp.where(lane == place_in, jnp.sum(folded, keepdims=True), row)
    sums[...] = jnp.broadcast_to(row, (GROUPS, CAP))


def widen_kernel(block, low_y, high_y, total, column, far_up, far_down):
    column[:32, :] = block[...]
    column[32:52, :] = low_y[4:24, :]
    column[52:72, :] = high_y[:20, :]
    column[72:76, :] = low_y[28:32, :]
    column[76:80, :] = total[0, 4:8, :]
    column[80:84, :] = total[YE - 1, 4:8, :]
    column[84:88, :] = high_y[24:28, :]
    for first, target in ((2, far_up), (0, far_down)):
        target[two(0), :] = low_y[20 + first : 22 + first, :]
        for y in range(8):
            target[two(1 + y), :] = block[4 * y + first : 4 * y + first + 2, :]
        target[two(9), :] = high_y[first : first + 2, :]
        for y in range(10):
            target[two(10 + y), :] = total[HALO - 1 + y, 4 + first : 6 + first, :]


def widen(block, low_y, high_y, total):
    return pl.pallas_call(
        widen_kernel,
        out_shape=[shape(88, DEPTH), shape(40, DEPTH), shape(40, DEPTH)],
        in_specs=[VM] * 4,
        out_specs=[VM] * 3,
        compiler_params=SMALL,
        name="widen",
    )(block, low_y, high_y, total)


def solve(edge, total, scaled, wide, basis_0, *inner):
    return pl.pallas_call(
        solve_kernel,
        out_shape=[shape(*BASIS)] * 5 + [shape(GROUPS, CAP)],
        in_specs=[SM] + [VM] * 12,
        out_specs=[VM] * 6,
        scratch_shapes=[pltpu.VMEM(BROAD, F32)] * 11
        + [pltpu.VMEM(BASIS, F32)]
        + [pltpu.VMEM(BLOCK, F32)] * 4,
        compiler_params=PARAMS,
        name="solve",
    )(edge, total, scaled, *wide, basis_0, *inner)


def coefficients(sums):
    total = jnp.sum(sums[...], axis=0, keepdims=True)
    g00, g01, g02, g11, g12, g22, b0, b1, b2 = [total[:, k : k + 1] for k in range(9)]
    l1 = g01 / g00
    l2 = g02 / g00
    d1 = g11 - l1 * g01
    keep_1 = d1 > 1e-7 * g11
    d1 = jnp.where(keep_1, d1, 1.0)
    m = jnp.where(keep_1, (g12 - l2 * g01) / d1, 0.0)
    d2 = g22 - l2 * g02 - m * m * d1
    keep_2 = d2 > 1e-7 * g22
    d2 = jnp.where(keep_2, d2, 1.0)
    y1 = b1 - l1 * b0
    y2 = b2 - l2 * b0 - m * y1
    c2 = jnp.where(keep_2, y2 / d2, 0.0)
    c1 = jnp.where(keep_1, y1 / d1, 0.0) - m * c2
    c0 = b0 / g00 - l1 * c1 - l2 * c2
    return c0, c1, c2


def gather_kernel(
    sums, basis_0, basis_1, basis_2, beta_x, beta_y, beta_z, own, msg,
    out, pressure_out, plane_s, depth_s, pressure, carried, table_s, hot_a, hot_b,
):
    c0, c1, c2 = [jnp.broadcast_to(c, (XE, DEPTH)) for c in coefficients(sums)]

    def combine(y):
        pressure[y] = c0 * basis_0[y] + c1 * basis_1[y] + c2 * basis_2[y]

    each_row(0, 10, combine)

    def slopes(y):
        here = pressure[y]
        flux_x = beta_x[y] * (here - next_x(here))
        flux_z = beta_z[y] * (here - next_z(here))
        flux_y = beta_y[y] * (here - pressure[y + 1])
        from_y = beta_y[y - 1] * (pressure[y - 1] - here)
        return (
            (flux_x + prev_x(flux_x)) * 0.5,
            (flux_y + from_y) * 0.5,
            (flux_z + prev_z(flux_z)) * 0.5,
            here,
        )

    targets = (carried.at[0], carried.at[1], carried.at[2], pressure_out)
    each_pair(1, lambda y: (targets, slopes(y), slopes(y + 1)))
    for axis in range(3):
        velocity = own[1 + axis]
        value = (velocity + carried[axis]) - FLIP * velocity
        for lift, level in ((0, value), (1, next_z(value))):
            first = axis * 64 + lift * CELLS
            table_s[first : first + CELLS, :] = level
            table_s[192 + first : 192 + first + CELLS, :] = remainder(level)
    cells_of(msg, plane_s, depth_s)
    level = lax.broadcasted_iota(jnp.int32, (DEPTH, CAP), 0)

    def build(chunk, hot):
        for j in range(PICK):
            depth_row = depth_s[pl.ds(chunk * PICK + j, 1), :]
            hot[:, j * CAP : (j + 1) * CAP] = jnp.where(level == depth_row, 1.0, 0.0)

    def pick(chunk, hot):
        both = one_pass(table_s[...], hot[...])
        table = both[:192] + both[192:]
        for j in range(PICK):
            source = chunk * PICK + j
            weights = tile_weights(msg, source, plane_s[pl.ds(source, 1), :])
            for axis in range(3):
                picked = table[axis * 64 : (axis + 1) * 64, j * CAP : (j + 1) * CAP] * weights
                out[pl.ds(3 * source + axis, 1), :] = jnp.sum(picked, axis=0, keepdims=True)

    turns = GROUPS // PICK
    build(0, hot_a)

    def body(turn, carry):
        build(2 * turn + 1, hot_b)
        pick(2 * turn, hot_a)
        build((2 * turn + 2) & (turns - 1), hot_a)
        pick(2 * turn + 1, hot_b)
        return carry

    lax.fori_loop(0, turns // 2, body, 0)


def gather(sums, bases, betas, own, msg):
    index = pltpu.VMEM((GROUPS, CAP), jnp.int32)
    hot = pltpu.VMEM((DEPTH, PICK * CAP), F32)
    return pl.pallas_call(
        gather_kernel,
        out_shape=[shape(3 * GROUPS, CAP), shape(*BLOCK)],
        in_specs=[VM] * 9,
        out_specs=[VM] * 2,
        scratch_shapes=[index, index, pltpu.VMEM(BASIS, F32), pltpu.VMEM((3,) + BLOCK, F32), pltpu.VMEM((384, DEPTH), F32), hot, hot],
        compiler_params=LARGE,
        name="gather",
    )(sums, *bases, *betas, own, msg)


def exchange(block, up, down, n_x, n_y, corner):
    up_x = [(i, (i + 1) % n_x) for i in range(n_x)]
    up_y = [(i, (i + 1) % n_y) for i in range(n_y)]
    down_x, down_y = [[(b, a) for a, b in up] for up in (up_x, up_y)]
    half = 4 * HALO
    low_y = lax.ppermute(up, "yz", up_y)
    high_y = lax.ppermute(down, "yz", down_y)
    near = 4 * corner
    near_low, near_high = low_y, high_y
    if corner < HALO:
        near_low, near_high = low_y[..., half - near :, :], high_y[..., :near, :]
    column = jnp.concatenate([block, near_low, near_high], axis=-2)
    return low_y, high_y, lax.ppermute(column, "gx", up_x), lax.ppermute(column, "gx", down_x)


def exchange_wide(block, up, down, total, n_x, n_y):
    up_x, up_xx = [[(i, (i + k) % n_x) for i in range(n_x)] for k in (1, 2)]
    up_y = [(i, (i + 1) % n_y) for i in range(n_y)]
    down_x, down_xx, down_y = [[(b, a) for a, b in pairs] for pairs in (up_x, up_xx, up_y)]
    low_y = lax.ppermute(up, "yz", up_y)
    high_y = lax.ppermute(down, "yz", down_y)
    column, far_up, far_down = widen(block, low_y, high_y, total)
    far_lx = lax.ppermute(far_up, "gx", up_xx)
    far_hx = lax.ppermute(far_down, "gx", down_xx)
    low_x = lax.ppermute(column, "gx", up_x)
    high_x = lax.ppermute(column, "gx", down_x)
    return low_y, high_y, low_x, high_x, far_lx, far_hx


def by_block(field):
    turned = jnp.swapaxes(field, -3, -2)
    return turned.reshape(turned.shape[:-3] + (CELLS, DEPTH))


def local(part_mass, part_vel, corner_weight, corner_base, slot_counts, water_vel, solid_flag):
    n_x, n_y = lax.axis_size("gx"), lax.axis_size("yz")
    at_x, at_y = lax.axis_index("gx"), lax.axis_index("yz")
    edge = jnp.stack(
        [at_x == 0, at_x == n_x - 1, at_y == 0, at_y == n_y - 1, at_x <= 1, at_x >= n_x - 2]
    ).astype(jnp.int32)
    velocity = jnp.swapaxes(part_vel[0], 0, 1)
    message = pack(
        part_mass[0], velocity, corner_weight.reshape(8 * GROUPS, CAP), corner_base[0], slot_counts
    )
    msg = lax.all_to_all(message.reshape(GROUPS, 1, FIELDS * CAP), ALL, 0, 0, tiled=True)
    msg = msg.reshape(GROUPS * FIELDS, CAP)
    density = by_block(jnp.where(solid_flag == 1, SOLID_WATER, 1.0).astype(F32))
    own, top, bottom = spread(msg, density, by_block(water_vel))
    near = exchange(own, top, bottom, n_x, n_y, CORNER)
    basis_0, own_0, image_0, scaled, source, total, up, down = start_solve(edge, own, near)
    wide = exchange_wide(scaled, up, down, total, n_x, n_y)
    basis_1, basis_2, *betas, sums = solve(
        edge, total, scaled, wide, basis_0, own_0, image_0, source
    )
    sums = lax.all_to_all(sums, ALL, 0, 0, tiled=True)
    sampled, pressure = gather(sums, (basis_0, basis_1, basis_2), betas, own, msg)
    returned = lax.all_to_all(sampled.reshape(GROUPS, 1, 3 * CAP), ALL, 0, 0, tiled=True)
    final = unpack(velocity, returned.reshape(3 * GROUPS, CAP))
    pressure = jnp.swapaxes(pressure.reshape(8, 4, DEPTH), 0, 1)
    return jnp.swapaxes(final, 0, 1)[None], pressure


def solution(mesh):
    parts = P(ALL, None, None)
    in_specs = (parts, P(ALL, None, None, None), P(ALL, None, None, None), parts, P(ALL, None), P(None, "gx", "yz", None), P("gx", "yz", None))
    out_specs = (P(ALL, None, None, None), P("gx", "yz", None))
    return jax.shard_map(local, mesh=mesh, in_specs=in_specs, out_specs=out_specs, check_vma=False)
```
